32 devices in a mesh: batch: 4 (over y, x), rows: 8 (over z, core).
Axes of the slice: x: 2, y: 2, z: 4, core: 2. Of those that a mesh axis runs over, the one named last changes fastest.
Arguments:
- features: bfloat16 [24, 128, 112, 128], P('batch', 'rows'), may hold values from -6 to 6
- cotangent: bfloat16 [24, 64, 112, 128], P('batch', 'rows'), may hold values from -6 to 6
- crop_ids: int32 [24, 64, 112], P('batch', 'rows'), may hold values from 0 to 447, as said below
- pooled_ids: int32 [24, 16, 28], P('batch', 'rows'), may hold values from 0 to 447, as said below
- master_weights: float32 [679936], P(('batch', 'rows')), as said below
- first_moment: float32 [679936], P(('batch', 'rows')), may hold values from -0.625 to 0.625
- second_moment: float32 [679936], P(('batch', 'rows')), may hold values from 0.001 to 0.004
- weight_average: float32 [679936], P(('batch', 'rows')), as said below
Outputs:
- layer_out: bfloat16 [24, 64, 112, 128], P('batch', 'rows')
- input_grad: float32 [24, 128, 112, 128], P('batch', 'rows')
- grad_norm: float32 [], replicated
- new_first: float32 [679936], P(('batch', 'rows'))
- new_second: float32 [679936], P(('batch', 'rows'))
- new_weights: float32 [679936], P(('batch', 'rows'))
- new_average: float32 [679936], P(('batch', 'rows'))
The draws below stay inside these ranges and needn't reach their ends.
Inputs may be any that keep to these rules, and one draw needn't show every extreme that they name: Each canvas is tiled by rectangular crops whose edges lie on multiples of 4 grid rows and columns; crop_ids gives each token its crop's number, distinct for distinct crops of a canvas; in every canvas one crop spans all 64 rows. pooled_ids[n, r, c] is the crop number of the tokens in rows 4r to 4r + 3 and columns 4c to 4c + 3 of canvas n. `master_weights`: matrices have entries of spread about one over the root of their fan-in, gains lie near one, biases are small. `weight_average`: drawn by the same law as master_weights.
All inputs are finite; a program needn't handle non-finite values.
Results may differ from the reference program's by a relative error of at most 0.015.
The reference program's roundings to bfloat16 on the way count: a program that leaves them out, or rounds other values in their place, can miss the bound.
Values may be sent and summed in bfloat16 or wider, within the bound.
No kernel may reach another device: no remote copies, remote signals or barrier semaphores. Data moves between devices by JAX's collectives and lax.ppermute only.
A program may use at most 256 MiB of HBM per device.

```python
import math
import jax
import jax.numpy as jnp
import numpy as np
from jax import lax

C_IN = 64
C = 128
HEADS = 2
FF = 1024
HEAD_DIM = 64
R = 8
W = 112
UPDATES = 10
H = 64
CANVASES = 24
NPAR_ALL = 679936


def crop_tables(key):
    base_key = jax.random.fold_in(key, 7)
    strip_key, band_key = jax.random.split(base_key)
    pool_rows = H // 4
    pool_cols = W // 4
    strip_cut = jax.random.randint(strip_key, (CANVASES, pool_cols), 0, 3) == 0
    strip_cut = strip_cut.at[:, 0].set(True)
    strip_cut = strip_cut.at[:, pool_cols - 1].set(True)
    col_index = jnp.broadcast_to(jnp.arange(pool_cols, dtype=jnp.int32)[None, :], (CANVASES, pool_cols))
    strip_start = lax.cummax(jnp.where(strip_cut, col_index, 0), axis=1)
    band_cut = jax.random.randint(band_key, (CANVASES, pool_cols, pool_rows), 0, 6) == 0
    band_cut = band_cut.at[:, :, 0].set(True)
    band_cut = band_cut.at[:, pool_cols - 1, pool_rows - 1].set(True)
    band_cut = band_cut.at[:, 0, :].set(jnp.arange(pool_rows) == 0)
    row_index = jnp.broadcast_to(jnp.arange(pool_rows, dtype=jnp.int32)[None, None, :], band_cut.shape)
    band_start = lax.cummax(jnp.where(band_cut, row_index, 0), axis=2)
    picked = jnp.take_along_axis(band_start, jnp.broadcast_to(strip_start[:, :, None], band_start.shape), axis=1)
    pooled = strip_start[:, :, None] * pool_rows + picked
    return jnp.transpose(pooled, (0, 2, 1)).astype(jnp.int32)


def draw_pooled_ids(key, part):
    return crop_tables(key)


def draw_crop_ids(key, part):
    pooled = crop_tables(key)
    return jnp.repeat(jnp.repeat(pooled, 4, axis=1), 4, axis=2)


def weight_scales():
    segments = [(9 * C_IN * C, (9 * C_IN) ** (-0.5), 0.0), (C, 0.1, 0.0), (C, 0.1, 1.0), (C, 0.1, 0.0), (C, 0.1, 1.0), (C, 0.1, 0.0), (C * C, 1.5 * C ** (-0.5), 0.0), (C, 0.1, 0.0), (C * C, 1.5 * C ** (-0.5), 0.0), (C * C, C ** (-0.5), 0.0), (C, 0.1, 0.0), (16 * C * C, (16 * C) ** (-0.5), 0.0), (C, 0.1, 0.0), (C, 0.1, 1.0), (C, 0.1, 0.0), (C * C, 3.0 * C ** (-0.5), 0.0), (C, 0.1, 0.0), (C, 0.1, 1.0), (C, 0.1, 0.0), (C * FF, C ** (-0.5), 0.0), (FF, 0.1, 0.0), (9 * FF, 1.0 / 3.0, 0.0), (FF, 0.1, 0.0), (FF * C, FF ** (-0.5), 0.0), (C, 0.1, 0.0)]
    used_count = sum((segment[0] for segment in segments))
    scale_tab = np.concatenate([np.full(segment[0], segment[1], np.float32) for segment in segments] + [np.full(NPAR_ALL - used_count, 0.02, np.float32)])
    shift_tab = np.concatenate([np.full(segment[0], segment[2], np.float32) for segment in segments] + [np.zeros(NPAR_ALL - used_count, np.float32)])
    return (scale_tab, shift_tab)


def weight_law(key):
    scale_tab, shift_tab = weight_scales()
    raw_noise = jax.random.normal(key, (NPAR_ALL,), jnp.float32)
    return raw_noise * jnp.asarray(scale_tab) + jnp.asarray(shift_tab)


def draw_master_weights(key, part):
    return weight_law(jax.random.fold_in(key, 11))


def draw_weight_average(key, part):
    return weight_law(jax.random.fold_in(key, 12))


def block_scale(stream_key, shape, cuts, least, high):
    factor_of, own = 1.0, jax.random.fold_in(stream_key, 6)
    for position, shards_of in cuts:
        heights = jnp.exp(jax.random.uniform(jax.random.fold_in(own, position), (shards_of,), jnp.float32, least / len(cuts), high / len(cuts)))
        factor_of = factor_of * jnp.repeat(heights, shape[position] // shards_of).reshape([-1 if axis == position else 1 for axis in range(len(shape))])
    return factor_of


def noise(rng, shape, deviation, bound, cuts=(), kind=jnp.bfloat16):
    array = jax.random.normal(rng, shape, jnp.float32) * deviation
    if len(cuts) > 0:
        array = block_scale(rng, shape, cuts, -0.22, 0.18) * array
    return jnp.clip(array, min=-bound, max=bound).astype(kind)


def setup_inputs(seed: int = 0) -> dict:
    streams_of = jax.random.split(jax.random.key(seed), 9)
    return {
        "features": noise(streams_of[0], (CANVASES, 2 * H, W, 2 * C_IN), 1.0, 6.0, ((0, 4), (1, 8))),
        "cotangent": noise(streams_of[1], (CANVASES, H, W, C), 1.0, 6.0, ((0, 4), (1, 8))),
        "crop_ids": draw_crop_ids(jax.random.fold_in(streams_of[8], 71), 0),
        "pooled_ids": draw_pooled_ids(jax.random.fold_in(streams_of[8], 71), 0),
        "master_weights": draw_master_weights(jax.random.fold_in(streams_of[8], 71), 0),
        "first_moment": noise(streams_of[5], (NPAR_ALL,), 0.11, 0.625, ((0, 32),), jnp.float32),
        "second_moment": jnp.clip(jnp.exp(math.log(0.004) - 1.3862944 * jax.random.uniform(streams_of[6], (NPAR_ALL,), jnp.float32) ** block_scale(streams_of[6], (NPAR_ALL,), ((0, 32),), -0.2, 0.2)), 0.001, 0.004),
        "weight_average": draw_weight_average(jax.random.fold_in(streams_of[8], 71), 0),
    }


@jax.custom_vjp
def low(v):
    return lax.optimization_barrier(v.astype(jnp.bfloat16)).astype(jnp.float32)

@jax.custom_vjp
def low_back(v):
    return v

def low_keep(v):
    return (low(v), None)

def low_pass(kept, grad):
    return (grad,)

def back_keep(v):
    return (v, None)

def back_low(kept, grad):
    return (low(grad),)
low.defvjp(low_keep, low_pass)
low_back.defvjp(back_keep, back_low)
NORM_EPS = 1e-06
BETA_ONE = 0.9
BETA_TWO = 0.999
LEARN_RATE = 0.1
DECAY_RATE = 0.05
ADAM_EPS = 1e-08
AVERAGE_KEEP = 0.9
MASKED = -1e+30
HIGHEST = lax.Precision.HIGHEST

def param_layout():
    return [('embed_w', (9 * C_IN, C)), ('embed_b', (C,)), ('embed_g', (C,)), ('embed_beta', (C,)), ('norm1_g', (C,)), ('norm1_b', (C,)), ('q_w', (C, C)), ('q_b', (C,)), ('k_w', (C, C)), ('v_w', (C, C)), ('v_b', (C,)), ('sr_w', (16 * C, C)), ('sr_b', (C,)), ('srn_g', (C,)), ('srn_b', (C,)), ('proj_w', (C, C)), ('proj_b', (C,)), ('norm2_g', (C,)), ('norm2_b', (C,)), ('fc1_w', (C, FF)), ('fc1_b', (FF,)), ('dw_w', (9, FF)), ('dw_b', (FF,)), ('fc2_w', (FF, C)), ('fc2_b', (C,))]

def unpack(flat_vec):
    pieces = {}
    offset = 0
    for name_key, shape_key in param_layout():
        number = math.prod(shape_key)
        pieces[name_key] = flat_vec[offset:offset + number].reshape(shape_key)
        offset += number
    return pieces

def product(left_arr, right_arr):
    return jnp.dot(left_arr, right_arr, precision=HIGHEST)

def layer_norm(value, gain, shift):
    centre = value - lax.optimization_barrier(jnp.mean(value, axis=-1, keepdims=True))
    spread = lax.optimization_barrier(jnp.mean(centre * centre, axis=-1, keepdims=True))
    return centre * lax.rsqrt(spread + NORM_EPS) * gain + shift

def gelu_exact(value):
    return 0.5 * value * (1.0 + lax.erf(value * 0.7071067811865476))

def same_masks(ids_ext, crop_map):
    grid_rows, grid_cols = (crop_map.shape[-2], crop_map.shape[-1])
    mask_tab = {}
    for row_off in (-1, 0, 1):
        for col_off in (-1, 0, 1):
            window = ids_ext[..., 1 + row_off:1 + row_off + grid_rows, 1 + col_off:1 + col_off + grid_cols]
            mask_tab[row_off, col_off] = (window == crop_map).astype(jnp.float32)
    return mask_tab

def embed_patches(extended, mask_tab, grid_rows):
    half_ch = extended.shape[-1] // 2
    collected = []
    for row_off in (-1, 0, 1):
        source = extended[..., row_off + 1:row_off + 1 + 2 * grid_rows:2, :, :]
        left_pad = jnp.zeros_like(source[..., :1, half_ch:])
        left_part = jnp.concatenate([left_pad, source[..., :-1, half_ch:]], axis=-2)
        top_off = min(row_off, 0)
        collected.append(left_part * mask_tab[top_off, -1][..., None].astype(source.dtype))
        collected.append(source * mask_tab[top_off, 0][..., None].astype(source.dtype))
    return jnp.concatenate(collected, axis=-1)

def depth_conv(hidden_ext, mask_tab, dw_weight, dw_bias):
    grid_rows = hidden_ext.shape[-3] - 2
    grid_cols = hidden_ext.shape[-2]
    widened = jnp.pad(hidden_ext, [(0, 0)] * (hidden_ext.ndim - 2) + [(1, 1), (0, 0)])
    running = jnp.zeros(widened.shape[:-3] + (grid_rows, grid_cols, widened.shape[-1]), jnp.float32) + dw_bias
    for row_off in (-1, 0, 1):
        for col_off in (-1, 0, 1):
            tap_index = 3 * (row_off + 1) + col_off + 1
            window = widened[..., 1 + row_off:1 + row_off + grid_rows, 1 + col_off:1 + col_off + grid_cols, :]
            running = running + mask_tab[row_off, col_off][..., None] * window.astype(jnp.float32) * dw_weight[tap_index]
    return running

def canvas_forward(flat_w, picture, crop_map, pooled_map, mask_tab):
    weights = unpack(flat_w)
    grid_rows, grid_cols = crop_map.shape
    extended = jnp.pad(picture, ((1, 0), (0, 0), (0, 0)))
    patches = embed_patches(extended, mask_tab, grid_rows)
    embedded = low_back(product(patches, weights['embed_w']) + weights['embed_b'])
    base_stream = layer_norm(embedded, weights['embed_g'], weights['embed_beta'])
    normed = low(layer_norm(base_stream, weights['norm1_g'], weights['norm1_b']))
    queries = low_back(low(product(normed, weights['q_w']) + weights['q_b']))
    blocks = normed.reshape(grid_rows // 4, 4, grid_cols // 4, 4, C).transpose(0, 2, 1, 3, 4).reshape(-1, 16 * C)
    reduced = low_back(product(blocks, weights['sr_w']) + weights['sr_b'])
    pooled = low(layer_norm(reduced, weights['srn_g'], weights['srn_b']))
    key_heads = low(product(pooled, weights['k_w'])).reshape(-1, HEADS, HEAD_DIM)
    value_heads = low(product(pooled, weights['v_w']) + weights['v_b']).reshape(-1, HEADS, HEAD_DIM)
    key_crop = pooled_map.reshape(-1)
    query_rows = queries.reshape(grid_rows // R, R * grid_cols, HEADS, HEAD_DIM)
    query_crop = crop_map.reshape(grid_rows // R, R * grid_cols)

    def attend(block_in):
        block_q, block_crop = block_in
        raw_scores = jnp.einsum('qhd,khd->hqk', block_q, key_heads, precision=HIGHEST)
        scores = low_back(raw_scores * HEAD_DIM ** (-0.5))
        masked = jnp.where((block_crop[:, None] == key_crop[None, :])[None], scores, MASKED)
        shifted = masked - lax.optimization_barrier(jnp.max(masked, axis=-1, keepdims=True))
        exp_scores = jnp.exp(shifted)
        prob_low = low(exp_scores / lax.optimization_barrier(jnp.sum(exp_scores, axis=-1, keepdims=True)))
        return jnp.einsum('hqk,khd->qhd', prob_low, value_heads, precision=HIGHEST)
    mixed_low = lax.map(jax.checkpoint(attend), (query_rows, query_crop))
    mixed_low = low_back(low(mixed_low.reshape(grid_rows, grid_cols, C)))
    attended = base_stream + low_back(product(mixed_low, weights['proj_w']) + weights['proj_b'])
    second = low(layer_norm(attended, weights['norm2_g'], weights['norm2_b']))
    hidden = low_back(low(product(second, weights['fc1_w']) + weights['fc1_b']))
    hidden_ext = jnp.pad(hidden, ((1, 1), (0, 0), (0, 0)))
    conv_out = low_back(depth_conv(hidden_ext, mask_tab, weights['dw_w'], weights['dw_b']))
    activated = low(gelu_exact(conv_out))
    return attended + low_back(product(activated, weights['fc2_w']) + weights['fc2_b'])

def reference(features, cotangent, crop_ids, pooled_ids, master_weights, first_moment, second_moment, weight_average):
    flat_low = low(master_weights)

    def one_canvas(grad_total, inputs):
        picture_in, grad_given, crop_map, pooled_map = inputs
        mask_tab = same_masks(jnp.pad(crop_map, 1, constant_values=-1), crop_map)

        def forward(flat_w, picture):
            return canvas_forward(flat_w, picture, crop_map, pooled_map, mask_tab)
        result, pullback = jax.vjp(forward, flat_low, picture_in.astype(jnp.float32))
        grad_flat, grad_picture = pullback(grad_given.astype(jnp.float32))
        return (grad_total + grad_flat, (result.astype(jnp.bfloat16), grad_picture))
    grad_total, outputs = lax.scan(one_canvas, jnp.zeros(master_weights.shape, jnp.float32), (features, cotangent, crop_ids, pooled_ids))
    layer_out, input_grad = outputs
    grad_norm = jnp.sqrt(jnp.sum(grad_total * grad_total))
    clip_limit = math.sqrt(NPAR_ALL)
    clipped = grad_total * (clip_limit / jnp.maximum(grad_norm, clip_limit))
    new_first = BETA_ONE * first_moment + (1.0 - BETA_ONE) * clipped
    new_second = BETA_TWO * second_moment + (1.0 - BETA_TWO) * clipped * clipped
    first_hat = new_first / (1.0 - BETA_ONE ** UPDATES)
    second_hat = new_second / (1.0 - BETA_TWO ** UPDATES)
    new_weights = master_weights * (1.0 - LEARN_RATE * DECAY_RATE) - LEARN_RATE * first_hat / (jnp.sqrt(second_hat) + ADAM_EPS)
    new_average = AVERAGE_KEEP * weight_average + (1.0 - AVERAGE_KEEP) * new_weights
    return (layer_out, input_grad, grad_norm, new_first, new_second, new_weights, new_average)
```

```python
import functools
import math

import jax
import jax.numpy as jnp
from jax import lax
from jax.experimental import pallas as pl
from jax.experimental.pallas import tpu as pltpu
from jax.sharding import PartitionSpec as P

C_IN = 64
C = 128
HEADS = 2
FF = 1024
HEAD_DIM = 64
UPDATES = 10

NORM_EPS = 1e-06
BETA_ONE = 0.9
BETA_TWO = 0.999
LEARN_RATE = 0.1
DECAY_RATE = 0.05
ADAM_EPS = 1e-08
AVERAGE_KEEP = 0.9
MASKED = -1e30
ROOT_HALF = 0.7071067811865476
LOG2E = 1.4426950408889634
PDF_SHIFT = math.log2(2.0 / math.sqrt(math.pi))
KEMB = 6 * C
K3 = 3 * C

f32 = jnp.float32
bf16 = jnp.bfloat16
VMEM_LIMIT = 60 * 2**20
SPARE = 32
MLP_PER = 1
EMBED_PER = 1
ATTEND_PER = 1
ATTEND_BACK_PER = 1
EMBED_BACK_PER = 1

VEC_NAMES = (
    "embed_b", "embed_g", "embed_beta", "norm1_g", "norm1_b", "q_b", "v_b", "sr_b",
    "srn_g", "srn_b", "proj_b", "norm2_g", "norm2_b", "fc2_b",
)
VEC = {name: i for i, name in enumerate(VEC_NAMES)}


def param_layout():
    return [
        ("embed_w", (9 * C_IN, C)),
        ("embed_b", (C,)),
        ("embed_g", (C,)),
        ("embed_beta", (C,)),
        ("norm1_g", (C,)),
        ("norm1_b", (C,)),
        ("q_w", (C, C)),
        ("q_b", (C,)),
        ("k_w", (C, C)),
        ("v_w", (C, C)),
        ("v_b", (C,)),
        ("sr_w", (16 * C, C)),
        ("sr_b", (C,)),
        ("srn_g", (C,)),
        ("srn_b", (C,)),
        ("proj_w", (C, C)),
        ("proj_b", (C,)),
        ("norm2_g", (C,)),
        ("norm2_b", (C,)),
        ("fc1_w", (C, FF)),
        ("fc1_b", (FF,)),
        ("dw_w", (9, FF)),
        ("dw_b", (FF,)),
        ("fc2_w", (FF, C)),
        ("fc2_b", (C,)),
    ]


def mm(left, right):
    return jnp.dot(left, right, preferred_element_type=f32)


def mm_nt(left, right):
    return lax.dot_general(
        left, right, (((1,), (1,)), ((), ())), preferred_element_type=f32
    )


def mm_tn(left, right):
    return lax.dot_general(
        left, right, (((0,), (0,)), ((), ())), preferred_element_type=f32
    )


def split_hi_lo(value):
    high = value.astype(bf16)
    return high, (value - high.astype(f32)).astype(bf16)


def normalise(value):
    centre = value - jnp.mean(value, axis=-1, keepdims=True)
    rstd = lax.rsqrt(jnp.mean(centre * centre, axis=-1, keepdims=True) + NORM_EPS)
    return centre * rstd, rstd


def normalise_back(grad, gain, xhat, rstd):
    scaled = grad * gain
    first = jnp.mean(scaled, axis=-1, keepdims=True)
    other = jnp.mean(scaled * xhat, axis=-1, keepdims=True)
    return rstd * (scaled - first - xhat * other)


def fold_rows(value):
    return jnp.sum(value.reshape(value.shape[0] // 8, 8, value.shape[1]), axis=0)


def lane_pad(count):
    return (count + C - 1) // C * C


def crop_columns(idr, grid_cols):
    ids = jnp.broadcast_to(idr[0], (8, idr.shape[2]))
    width = ids.shape[1]
    column = lax.broadcasted_iota(jnp.int32, ids.shape, 1) % grid_cols
    kind = lax.broadcasted_iota(jnp.int32, ids.shape, 0)
    left = (ids == pltpu.roll(ids, 1, 1)) & (column != 0)
    right = (ids == pltpu.roll(ids, width - 1, 1)) & (column != grid_cols - 1)
    upper = ids == pltpu.roll(ids, grid_cols, 1)
    lower = ids == pltpu.roll(ids, width - grid_cols, 1)
    rows = jnp.zeros(ids.shape, f32)
    for k, same in enumerate((left, right, upper, lower)):
        rows = jnp.where((kind == k) & same, 1.0, rows)
    return rows.T


def spread(columns, k, start, count):
    return jnp.broadcast_to(columns[start : start + count, k : k + 1], (count, C))


def tap_rows(idr, grid_cols):
    ids = jnp.broadcast_to(idr[0], (32, idr.shape[2]))
    width = ids.shape[1]
    column = lax.broadcasted_iota(jnp.int32, ids.shape, 1) % grid_cols
    kind = lax.broadcasted_iota(jnp.int32, ids.shape, 0) % 16
    rows = jnp.where(kind == 9, 1.0, jnp.zeros(ids.shape, f32))
    for a in (-1, 0, 1):
        for b in (-1, 0, 1):
            k = 3 * (a + 1) + b + 1
            away = (-(a * grid_cols + b)) % width
            same = ids == (pltpu.roll(ids, away, 1) if away else ids)
            inside = (column + b >= 0) & (column + b < grid_cols)
            rows = jnp.where((kind == k) & same & inside, 1.0, rows)
    return pltpu.roll(rows, width - grid_cols, 1)


def one_hot_digits(low, high):
    lane = lax.broadcasted_iota(jnp.int32, (low.shape[0], C), 1).astype(f32)
    return (lane == low) | (lane == high + 32.0)


def when_first(starts):
    def run(body):
        if starts:
            pl.when(pl.program_id(0) == 0)(body)

    return run


class Stack:
    def __init__(self, value):
        self.value = value
        self.shape = value.shape


class Whole:
    def __init__(self, value):
        self.value = value
        self.shape = value.shape


class Held:
    def __init__(self, value, behind=False):
        self.value, self.behind = value, behind
        self.shape = value.shape


class Group:
    def __init__(self, count, first, per=1):
        self.count, self.first, self.per = count, first, per


def canvas_block(array, group):
    shape, per = array.shape, group.per
    at = group.first // per if isinstance(array, Whole) else 0
    if isinstance(array, Held):
        return pl.BlockSpec(memory_space=pltpu.VMEM)
    if isinstance(array, Stack):
        return pl.BlockSpec((shape[0], per) + shape[2:], lambda i: (0, i) + (0,) * (len(shape) - 2))
    return pl.BlockSpec((per,) + shape[1:], lambda i: (i + at,) + (0,) * (len(shape) - 1))


def bare(array):
    return array.value if isinstance(array, (Stack, Whole, Held)) else array


def whole_block(shape):
    return pl.BlockSpec(shape, lambda i: (0,) * len(shape))


def per_canvas_call(
    kernel, name, group, canvas_in, shared_in, canvas_out, shared_out, scratch, flops=0, earlier=(),
    inside=False,
):
    steps = group.count // group.per
    inputs = [
        pltpu.with_memory_space_constraint(x.value, pltpu.VMEM) if isinstance(x, Held) else bare(x)
        for x in canvas_in
    ] + list(shared_in)
    outputs = [bare(x) for x in canvas_out] + list(shared_out)
    in_specs = [canvas_block(x, group) for x in canvas_in]
    in_specs += [
        pl.BlockSpec(memory_space=pltpu.SMEM) if x.ndim == 1 else whole_block(x.shape)
        for x in shared_in
    ]
    aliases = {}
    if earlier:
        aliases = {len(inputs) + k: place for k, (place, _) in enumerate(earlier)}
        skip = slice(len(inputs), len(inputs) + len(earlier))
        in_specs += [pl.BlockSpec(memory_space=pl.ANY)] * len(earlier)
        inputs += [array for _, array in earlier]

    else:
        skip = slice(len(inputs), len(inputs))

    def body(*refs):
        refs = list(refs[: skip.start] + refs[skip.stop :])
        out_at = len(canvas_in) + len(shared_in)
        per_canvas = list(enumerate(canvas_in)) + [
            (out_at + k, x) for k, x in enumerate(canvas_out)
        ]
        if inside:
            views = list(refs)
            for k, x in per_canvas:
                if isinstance(x, Held):
                    views[k] = refs[k].at[pl.ds(pl.program_id(0) * group.per, group.per)]
            kernel(*views)
            return
        for p in range(group.per):
            views = list(refs)
            for k, x in per_canvas:
                behind = isinstance(x, Stack) or (isinstance(x, Held) and x.behind)
                at = pl.ds(pl.program_id(0) * group.per + p, 1) if isinstance(x, Held) else pl.ds(p, 1)
                views[k] = refs[k].at[:, at] if behind else refs[k].at[at]
            kernel(p == 0, p == group.per - 1, *views)

    bytes_moved = sum(x.size * x.dtype.itemsize for x in inputs) + sum(
        math.prod(x.shape) * x.dtype.itemsize for x in outputs
    )
    return pl.pallas_call(
        body,
        grid=(steps,),
        in_specs=in_specs,
        out_specs=[canvas_block(x, group) for x in canvas_out]
        + [whole_block(x.shape) for x in shared_out],
        out_shape=outputs,
        scratch_shapes=scratch,
        input_output_aliases=aliases,
        compiler_params=pltpu.CompilerParams(vmem_limit_bytes=VMEM_LIMIT),
        cost_estimate=pl.CostEstimate(
            flops=int(flops * group.count), bytes_accessed=int(bytes_moved), transcendentals=0
        ),
        name=name,
    )(*inputs)


def near_masks_kernel(grid_rows, grid_cols, starts, ends, idr, hm_out, vm_out):
    columns = crop_columns(idr, grid_cols)
    extended = (grid_rows + 2) * grid_cols
    for k in range(2):
        hm_out[0, k] = spread(columns, k, 0, extended).astype(bf16)
    for r in range(0, grid_rows, 4):
        k = 2 * (r // 4)
        vm_out[0, k] = spread(columns, 2, (r + 1) * grid_cols, grid_cols).astype(bf16)
        vm_out[0, k + 1] = spread(columns, 3, (r + 4) * grid_cols, grid_cols).astype(bf16)


def near_masks_call(group, grid_rows, grid_cols, idr):
    canvases = idr.shape[0]
    sds = jax.ShapeDtypeStruct
    return per_canvas_call(
        functools.partial(near_masks_kernel, grid_rows, grid_cols),
        "near_masks",
        group,
        [idr],
        [],
        [
            sds((canvases, 2, (grid_rows + 2) * grid_cols, C), bf16),
            sds((canvases, grid_rows // 2, grid_cols, C), bf16),
        ],
        [],
        [],
    )


def token_masks_kernel(grid_cols, starts, ends, idr, hot_out, aug_out, row_out):
    tokens = hot_out.shape[1]
    ids = jnp.broadcast_to(idr[0], (8, idr.shape[2]))
    kind = lax.broadcasted_iota(jnp.int32, ids.shape, 0)
    column = jnp.where(kind == 0, ids % 32, ids // 32).astype(f32).T
    column = column[grid_cols : grid_cols + tokens]
    hot = one_hot_digits(column[:, 0:1], column[:, 1:2])
    hot_out[0] = jnp.where(hot, 1.0, 0.0).astype(bf16)
    taps = tap_rows(idr, grid_cols)
    for q in range(2):
        rows = [taps[:, r * grid_cols : (r + 1) * grid_cols] for r in range(q, tokens // grid_cols, 2)]
        row_out[0, q] = jnp.concatenate(rows, axis=1).astype(bf16)
    aug_out[0, :, 0:32] = taps.T[:tokens].astype(bf16)
    aug_out[0, :, 32:] = jnp.zeros((tokens, C - 32), bf16)


def token_masks_call(group, grid_rows, grid_cols, idr):
    canvases, tokens = idr.shape[0], grid_rows * grid_cols
    sds = jax.ShapeDtypeStruct
    return per_canvas_call(
        functools.partial(token_masks_kernel, grid_cols),
        "token_masks",
        group,
        [idr],
        [],
        [
            sds((canvases, tokens, C), bf16),
            sds((canvases, tokens, C), bf16),
            sds((canvases, 2, 32, tokens // 2), bf16),
        ],
        [],
        [],
    )


def fill_patches(grid_rows, grid_cols, feat, rim, hm, vm, patches):
    tokens = grid_rows * grid_cols
    left = hm[0, 0]
    for a in range(3):
        rows = []
        for r in range(grid_rows):
            if a == 0:
                rows.append(rim[0] if r == 0 else feat[0, r - 1, 1])
            else:
                rows.append(feat[0, r, a - 1])
        source = jnp.concatenate(rows, axis=0)
        rolled = pltpu.roll(source.astype(f32), 1, 0)
        mask_at = 0 if a == 0 else grid_cols
        shifted = (rolled * left[mask_at : mask_at + tokens].astype(f32)).astype(bf16)
        if a == 0:
            for r in range(grid_rows):
                here = slice(r * grid_cols, (r + 1) * grid_cols)
                if r % 4 == 0:
                    keep = vm[0, 2 * (r // 4)]
                    patches[here, 0:C] = source[here] * keep
                    patches[here, 3 * C : 4 * C] = shifted[here] * keep
                else:
                    patches[here, 0:C] = source[here]
                    patches[here, 3 * C : 4 * C] = shifted[here]
        else:
            patches[:, a * C : (a + 1) * C] = source
            patches[:, (3 + a) * C : (4 + a) * C] = shifted


def embed_kernel(
    grid_rows, grid_cols, starts, ends,
    feat, rim, hm, vm, own_ids, vecs, embed_w, q_w, sr_w,
    emb_out, base_out, norm_out, q_out, blk_out, red_out, pool_out, patch_out,
    tok, blkf,
):
    pool_rows, pool_cols = grid_rows // 4, grid_cols // 4
    patches = patch_out.at[0]
    fill_patches(grid_rows, grid_cols, feat, rim, hm, vm, patches)
    vec = lambda name: vecs[VEC[name] : VEC[name] + 1, :]
    embedded = mm(patches[...], embed_w[...]) + vec("embed_b")
    emb_out[0] = embedded
    base = normalise(embedded)[0] * vec("embed_g") + vec("embed_beta")
    base_out[0] = base
    normed = (normalise(base)[0] * vec("norm1_g") + vec("norm1_b")).astype(bf16)
    norm_out[0] = normed
    queries = (mm(normed, q_w[...]) + vec("q_b")).astype(bf16)
    q_out[0] = queries * bf16(HEAD_DIM ** (-0.5))
    tok[0 : normed.shape[0], :] = normed.astype(f32)
    for r in range(pool_rows):
        for di in range(4):
            for dj in range(4):
                k = 4 * di + dj
                start = (4 * r + di) * grid_cols + dj
                blkf[r * pool_cols : (r + 1) * pool_cols, k * C : (k + 1) * C] = tok[
                    pl.ds(start, pool_cols, stride=4), :
                ]
    blocks = blkf[0 : pool_rows * pool_cols, :].astype(bf16)
    blk_out[0] = blocks
    reduced = mm(blocks, sr_w[...]) + vec("sr_b")
    red_out[0] = reduced
    own = pool_rows * pool_cols
    pooled = normalise(reduced)[0] * vec("srn_g") + vec("srn_b")
    ids = jnp.broadcast_to(own_ids[0], (8, C))
    kind = lax.broadcasted_iota(jnp.int32, ids.shape, 0)
    digits = jnp.where(kind == 0, ids % 32, jnp.where(kind == 1, ids // 32, 0)).astype(f32)
    pool_out[0] = jnp.concatenate([pooled, digits], axis=0).astype(bf16)


def embed_call(group, feat, rim, hm, vm, own_ids, vecs, embed_w, q_w, sr_w):
    canvases = group.count
    _, grid_rows, _, grid_cols, _ = feat.shape
    tokens = grid_rows * grid_cols
    own = tokens // 16
    sds = jax.ShapeDtypeStruct
    return per_canvas_call(
        functools.partial(embed_kernel, grid_rows, grid_cols),
        "embed",
        group,
        [Whole(feat), Held(rim), Whole(hm), Whole(vm), Whole(own_ids)],
        [vecs, embed_w, q_w, sr_w],
        [
            sds((canvases, tokens, C), f32),
            sds((canvases, tokens, C), f32),
            sds((canvases, tokens, C), bf16),
            sds((canvases, tokens, C), bf16),
            sds((canvases, own, 16 * C), bf16),
            sds((canvases, own, C), f32),
            sds((canvases, own + 8, C), bf16),
            sds((canvases, tokens, KEMB), bf16),
        ],
        [],
        [
            pltpu.VMEM((tokens + SPARE, C), f32),
            pltpu.VMEM((own + 8, 16 * C), f32),
        ],
        flops=2e9,
    )


def keys_values(pooled, kv_w, vecs):
    both = mm(pooled, kv_w)
    keys = both[:, :C].astype(bf16)
    values = (both[:, C:] + vecs[VEC["v_b"] : VEC["v_b"] + 1, :]).astype(bf16)
    return keys, values


def head_lanes(shape, head):
    lane = lax.broadcasted_iota(jnp.int32, shape, 1)
    return (lane // HEAD_DIM) == head


def all_pooled_rows(near, far):
    own = near.shape[2] - 8
    parts = [ref[k, 0].astype(f32) for ref in (near, far) for k in range(ref.shape[0])]
    return jnp.concatenate([part[:own] for part in parts], axis=0), [p[own:] for p in parts]


def attend_kernel(
    starts, ends,
    q, near, far, q_hot, base, vecs, kv_w, proj_w,
    exp_out, mix_out, inv_out, att_out, sec_out, head_out, tail_out,
):
    vec = lambda name: vecs[VEC[name] : VEC[name] + 1, :]
    pooled, digits = all_pooled_rows(near, far)
    keys, values = keys_values(pooled.astype(bf16), kv_w[...], vecs)
    values_t = values.astype(f32).T.astype(bf16)
    tokens = q.shape[1]
    own = near.shape[2] - 8
    hot = []
    for part in digits:
        column = part.T
        hot.append(one_hot_digits(column[:own, 0:1], column[:own, 1:2]))
    k_hot = jnp.where(jnp.concatenate(hot, axis=0), 0.0, MASKED).astype(bf16)
    q_cat = jnp.concatenate([q[0], q_hot[0]], axis=1)
    for h in range(HEADS):
        k_own = jnp.where(head_lanes(keys.shape, h), keys, jnp.zeros_like(keys))
        scores = mm_nt(jnp.concatenate([k_own, k_hot], axis=1), q_cat)
        peak = jnp.max(scores, axis=0, keepdims=True)
        raised = jnp.exp(scores - peak)
        inverse = 1.0 / jnp.sum(raised, axis=0, keepdims=True)
        low = raised.astype(bf16)
        exp_out[0, h] = low
        inv_out[0, 4 * h : 4 * h + 4, :] = jnp.broadcast_to(inverse, (4, tokens))
        part = slice(h * HEAD_DIM, (h + 1) * HEAD_DIM)
        mix_out[0, part, :] = mm(values_t[part], low) * inverse
    mixed = mix_out[0].T.astype(bf16)
    attended = base[0] + mm(mixed, proj_w[...]) + vec("proj_b")
    att_out[0] = attended
    second = (normalise(attended)[0] * vec("norm2_g") + vec("norm2_b")).astype(bf16)
    sec_out[0] = second
    grid_cols = head_out.shape[1]
    head_out[0] = second[:grid_cols]
    tail_out[0] = second[tokens - grid_cols :]


def attend_call(group, grid_cols, q, near, far, q_hot, base, vecs, kv_w, proj_w):
    canvases, tokens, _ = q.shape
    total = 2 * near.shape[0] * (near.shape[2] - 8)
    sds = jax.ShapeDtypeStruct
    return per_canvas_call(
        attend_kernel,
        "attend",
        group,
        [q, Held(near, True), Held(far, True), Whole(q_hot), base],
        [vecs, kv_w, proj_w],
        [
            sds((canvases, HEADS, total, tokens), bf16),
            sds((canvases, C, tokens), f32),
            sds((canvases, 8, tokens), f32),
            sds((canvases, tokens, C), f32),
            sds((canvases, tokens, C), bf16),
            sds((canvases, grid_cols, C), bf16),
            sds((canvases, grid_cols, C), bf16),
        ],
        [],
        [],
        flops=2.5e9,
    )


def attend_back_kernel(
    grid_cols, starts, ends,
    gsec, gtop, gbot, att, cot, mix, inv, exp_in, q, normed, near, far, vecs, kv_w, proj_w,
    gatt_out, gq_out, gnear_out, gfar_out, gproj_out, gkv_out, gqw_out, gvec_out,
):
    step = pl.program_id(0)
    vec = lambda name: vecs[VEC[name] : VEC[name] + 1, :]

    @when_first(starts)
    def _():
        gproj_out[...] = jnp.zeros_like(gproj_out)
        gkv_out[...] = jnp.zeros_like(gkv_out)
        gqw_out[...] = jnp.zeros_like(gqw_out)
        gvec_out[...] = jnp.zeros_like(gvec_out)

    tokens = q.shape[1]
    last = tokens - grid_cols
    grad_second = jnp.concatenate(
        [
            gsec[0, :grid_cols] + gtop[0].astype(f32),
            gsec[0, grid_cols:last],
            gsec[0, last:] + gbot[0].astype(f32),
        ],
        axis=0,
    )
    xhat, rstd = normalise(att[0])
    gvec_out[0] += fold_rows(grad_second * xhat)
    gvec_out[1] += fold_rows(grad_second)
    grad_att = cot[0].astype(f32) + normalise_back(grad_second, vec("norm2_g"), xhat, rstd)
    gatt_out[0] = grad_att
    branch = grad_att.astype(bf16)
    gvec_out[2] += fold_rows(branch.astype(f32))
    mixed_t = mix[0]
    gproj_out[...] += mm(mixed_t.astype(bf16), branch)
    grad_mix_t = mm_nt(proj_w[...], branch)
    inverses = inv[0]
    pooled_f, _ = all_pooled_rows(near, far)
    keys, values = keys_values(pooled_f.astype(bf16), kv_w[...], vecs)
    keys_t = keys.astype(f32).T.astype(bf16)
    gq_parts = []
    gk_parts = []
    gv_parts = []
    for h in range(HEADS):
        part = slice(h * HEAD_DIM, (h + 1) * HEAD_DIM)
        scaled = (grad_mix_t[part] * inverses[4 * h : 4 * h + 1]).astype(bf16)
        middle = jnp.sum(scaled.astype(f32) * mixed_t[part], axis=0, keepdims=True)
        raised = exp_in[0, h]
        pair = jnp.concatenate([scaled, scaled], axis=0)
        gv_parts.append(mm_nt(raised, pair))
        v_own = jnp.where(head_lanes(values.shape, h), values, jnp.zeros_like(values))
        grad_p = mm(v_own, pair)
        grad_s = (raised.astype(f32) * (grad_p - middle)).astype(bf16)
        gq_parts.append(mm(keys_t[part], grad_s))
        gk_parts.append(mm(grad_s, q[0]))
    first = head_lanes(gk_parts[0].shape, 0)
    grad_keys = jnp.where(first, gk_parts[0], gk_parts[1])
    grad_values = jnp.where(first, gv_parts[0], gv_parts[1])
    grad_q = (jnp.concatenate(gq_parts, axis=0) * HEAD_DIM ** (-0.5)).T.astype(bf16)
    gq_out[0] = grad_q
    gvec_out[3] += fold_rows(grad_q.astype(f32))
    gvec_out[4] += fold_rows(grad_values)
    gqw_out[...] += mm_tn(normed[0], grad_q)
    k_high, k_low = split_hi_lo(grad_keys)
    v_high, v_low = split_hi_lo(grad_values)
    high = jnp.concatenate([k_high, v_high], axis=1)
    low = jnp.concatenate([k_low, v_low], axis=1)
    pooled_t = pooled_f.T.astype(bf16)
    gkv_out[...] += mm(pooled_t, high) + mm(pooled_t, low)
    grad_pool = mm_nt(high, kv_w[...]) + mm_nt(low, kv_w[...])
    chain, own = near.shape[0], near.shape[2] - 8
    for k in range(chain):
        gnear_out[k, 0] = grad_pool[k * own : (k + 1) * own].astype(bf16)
        gfar_out[k, 0] = grad_pool[(chain + k) * own : (chain + k + 1) * own].astype(bf16)


def attend_back_call(
    group, gsec, gtop, gbot, att, cot, mix, inv, exp_in, q, normed, near, far, vecs, kv_w, proj_w
):
    canvases, tokens, _ = q.shape
    sds = jax.ShapeDtypeStruct
    gpool = sds((near.shape[0], canvases, near.shape[2] - 8, C), bf16)
    return per_canvas_call(
        functools.partial(attend_back_kernel, gtop.shape[1]),
        "attend_back",
        group,
        [
            gsec, Held(gtop), Held(gbot), att, Whole(cot), mix, inv, exp_in, q, normed,
            Held(near, True), Held(far, True),
        ],
        [vecs, kv_w, proj_w],
        [
            sds((canvases, tokens, C), f32),
            sds((canvases, tokens, C), bf16),
            Stack(gpool),
            Stack(gpool),
        ],
        [
            sds((C, C), f32),
            sds((C, 2 * C), f32),
            sds((C, C), f32),
            sds((5, 8, C), f32),
        ],
        [],
        flops=3.5e9,
    )


def mlp_kernel(
    grid_rows, grid_cols,
    sec, top, bot, hm, vm, aug, aug_rows, cot, att, fc1, dwv, fc2h, vecs,
    lo, gsec, gtop, gbot, gfc1, gdw, gfc2t, gfc2b,
    wf, wt, f2t, xf, xt, acc, ones_grad, act, gm, gx,
):
    tokens = grid_rows * grid_cols
    half = tokens // 2
    pairs = grid_rows // 2
    extended = tokens + 2 * grid_cols
    step = pl.program_id(0)
    per = sec.shape[0]

    @pl.when(step == 0)
    def _():
        first = fc1[...].astype(f32)
        for b in range(3):
            rows = [first * (dwv[3 * a + b : 3 * a + b + 1, :] * ROOT_HALF) for a in range(3)]
            ends = (rows[0] + rows[2]) * 0.5
            mixed = [rows[0], ends + rows[1] * 0.5, ends - rows[1] * 0.5, rows[2]]
            for k in range(4):
                wf[k, b * C : (b + 1) * C, :] = mixed[k].astype(bf16)
        high, low = split_hi_lo(dwv[0:16, :] * dwv[16:32, :] * ROOT_HALF)
        for k in (0, 3):
            wf[k, K3 : K3 + 16, :] = high
            wf[k, K3 + 16 : K3 + 32, :] = low
            wf[k, K3 + 32 :, :] = jnp.zeros((C - 32, FF), bf16)
        for k in range(4):
            wt[k] = wf[k, :K3, :].T
        f2t[...] = fc2h[...].T
        acc[...] = jnp.zeros_like(acc)
        ones_grad[...] = jnp.zeros_like(ones_grad)
        gfc2t[...] = jnp.zeros_like(gfc2t)
        gfc2b[...] = jnp.zeros_like(gfc2b)

    def row(r):
        return slice(r * grid_cols, (r + 1) * grid_cols)

    def upper(r, p):
        return vm[p, 2 * (r // 4)].astype(f32) if r % 4 == 0 else None

    def lower(r, p):
        return vm[p, 2 * (r // 4) + 1].astype(f32) if r % 4 == 3 else None

    def kept(value, mask):
        return value if mask is None else value * mask

    for p in range(per):
        wide = jnp.concatenate(
            [top[p].astype(f32), sec[p].astype(f32), bot[p].astype(f32)], axis=0
        )
        for b in range(3):
            moved = wide
            if b != 1:
                moved = pltpu.roll(wide, 1 if b == 0 else extended - 1, 0)
                moved = moved * hm[p, b // 2].astype(f32)
            for i in range(pairs):
                d0, d1, d2, d3 = [moved[row(2 * i + k)] for k in range(4)]
                d0, d3 = kept(d0, upper(2 * i, p)), kept(d3, lower(2 * i + 1, p))
                at = slice(p * half + i * grid_cols, p * half + (i + 1) * grid_cols)
                for k, value in enumerate((d0 - d2, d1 + d2, d2 - d1, d1 - d3)):
                    xf[k, at, b * C : (b + 1) * C] = value.astype(bf16)
        mine = slice(p * half, (p + 1) * half)
        for k in range(4):
            xt[k, :, mine] = xf[k, mine, :K3].T
        for i in range(pairs):
            at = slice(p * half + i * grid_cols, p * half + (i + 1) * grid_cols)
            xf[0, at, K3:] = aug[p, row(2 * i)]
            xf[3, at, K3:] = -aug[p, row(2 * i + 1)]

    def by_parity(ref):
        return jnp.concatenate(
            [ref[p, row(2 * i + q)] for q in range(2) for p in range(per) for i in range(pairs)],
            axis=0,
        )

    given = by_parity(cot)
    m0 = mm(xf[0], wf[0])
    m1 = mm(xf[1, :, :K3], wf[1, :K3])
    m2 = mm(xf[2, :, :K3], wf[2, :K3])
    m3 = mm(xf[3], wf[3])
    d = mm(given, f2t[...])
    grads = []
    for q, u in enumerate((m0 + (m1 + m2), (m1 - m2) - m3)):
        at = slice(q * per * half, (q + 1) * per * half)
        phi = 1.0 + lax.erf(u)
        act[at, :] = (u * phi).astype(bf16)
        pdf = jnp.exp2(PDF_SHIFT - u * u * LOG2E)
        grads.append((phi + u * pdf) * d[at])
    even, odd = grads
    for k, value in enumerate((even, even + odd, even - odd, -odd)):
        gm[k] = value.astype(bf16)
    for k in range(4):
        acc[k] += mm(xt[k], gm[k])
        gx[k] = mm(gm[k], wt[k])
    for q in range(2):
        taps = jnp.concatenate([aug_rows[p, q] for p in range(per)], axis=1)
        ones_grad[...] += mm(taps, gm[3 * q] if q == 0 else -gm[3])
    given_f = given.astype(f32)
    gfc2t[...] += mm(given_f.T.astype(bf16), act[...])
    gfc2b[...] += fold_rows(given_f)
    mlp_out = mm(act[...], fc2h[...]) * (2 * ROOT_HALF) + vecs[VEC["fc2_b"] : VEC["fc2_b"] + 1, :]
    for p in range(per):
        total = None
        for b in range(3):
            rows = [None] * (grid_rows + 2)
            lanes = slice(b * C, (b + 1) * C)
            for i in range(pairs):
                at = slice(p * half + i * grid_cols, p * half + (i + 1) * grid_cols)
                c0, c1, c2, c3 = [gx[k, at, lanes] for k in range(4)]
                d0, d3 = kept(c0, upper(2 * i, p)), kept(-c3, lower(2 * i + 1, p))
                for k, value in enumerate((d0, (c1 - c2) + c3, (c1 + c2) - c0, d3)):
                    e = 2 * i + k
                    rows[e] = value if rows[e] is None else rows[e] + value
            side = jnp.concatenate(rows, axis=0)
            if b != 1:
                side = pltpu.roll(
                    side * hm[p, b // 2].astype(f32), extended - 1 if b == 0 else 1, 0
                )
            total = side if total is None else total + side
        total = total * (2 * ROOT_HALF)
        gtop[p] = total[0:grid_cols].astype(bf16)
        gsec[p] = total[grid_cols : grid_cols + tokens]
        gbot[p] = total[grid_cols + tokens :].astype(bf16)
        for i in range(pairs):
            for q in range(2):
                at = (q * per + p) * half + i * grid_cols
                r = row(2 * i + q)
                lo[p, r] = (att[p, r] + mlp_out[at : at + grid_cols]).astype(bf16)

    @pl.when(step == pl.num_programs(0) - 1)
    def _():
        first = fc1[...].astype(f32)
        summed = None
        bias = ones_grad[0:16, :]
        for b in range(3):
            lanes = slice(b * C, (b + 1) * C)
            both = (acc[1, lanes, :] + acc[2, lanes, :]) * 0.5
            apart = (acc[1, lanes, :] - acc[2, lanes, :]) * 0.5
            for a, tap in enumerate((acc[0, lanes, :] + both, apart, acc[3, lanes, :] + both)):
                k = 3 * a + b
                term = tap * dwv[k : k + 1, :]
                summed = term if summed is None else summed + term
                gdw[k : k + 1, :] = (
                    jnp.sum(tap * first, axis=0, keepdims=True) + bias[k : k + 1] * dwv[16:17, :]
                )
        gfc1[...] = summed
        gdw[9:10, :] = bias[9:10]
        gdw[10:11, :] = jnp.sum(bias[0:9] * dwv[0:9, :], axis=0, keepdims=True)
        gdw[11:16, :] = jnp.zeros((5, FF), f32)
        gfc2t[...] = gfc2t[...] * ROOT_HALF


def mlp_call(
    group, sec, top, bot, hm, vm, aug, aug_rows, cot, att, fc1, dwv, fc2h, vecs, earlier
):
    canvases, tokens, _ = sec.shape
    grid_cols = top.shape[1]
    grid_rows = tokens // grid_cols
    stacked = group.per * tokens
    sds = jax.ShapeDtypeStruct
    vmem = pltpu.VMEM
    return per_canvas_call(
        functools.partial(mlp_kernel, grid_rows, grid_cols),
        "feed_forward",
        group,
        [
            sec, Held(top), Held(bot), Whole(hm), Whole(vm), Whole(aug), Whole(aug_rows), Whole(cot), att,
        ],
        [fc1, dwv, fc2h, vecs],
        [
            Whole(sds(cot.shape, bf16)),
            sds((canvases, tokens, C), f32),
            sds((canvases, grid_cols, C), bf16),
            sds((canvases, grid_cols, C), bf16),
        ],
        [
            sds((C, FF), f32),
            sds((16, FF), f32),
            sds((C, FF), f32),
            sds((8, C), f32),
        ],
        [
            vmem((4, K3 + C, FF), bf16),
            vmem((4, FF, K3), bf16),
            vmem((C, FF), bf16),
            vmem((4, stacked // 2, K3 + C), bf16),
            vmem((4, K3, stacked // 2), bf16),
            vmem((4, K3, FF), f32),
            vmem((32, FF), f32),
            vmem((stacked, FF), bf16),
            vmem((4, stacked // 2, FF), bf16),
            vmem((4, stacked // 2, K3), f32),
        ],
        flops=9e9,
        earlier=[(0, x) for x in earlier],
        inside=True,
    )


def embed_back_kernel(
    grid_rows, grid_cols, parts, starts, ends,
    *refs,
):
    gpool = refs[:parts]
    (
        red, emb, gatt, gq, blk, patches, hm, vm, vecs, embed_w, q_w, sr_w,
        slots, gvec_att, gqw, gkv, gproj, gfc1, gdw, gfc2t, gfc2b,
    ) = refs[parts : parts + 21]
    gin_out, grim_out, own_out, *other_out = refs[parts + 21 : -6]
    un, pg, gsr_out, gemb_out, gvec_out, flat = refs[-6:]
    step = pl.program_id(0)
    pool_rows, pool_cols = grid_rows // 4, grid_cols // 4
    tokens = grid_rows * grid_cols
    vec = lambda name: vecs[VEC[name] : VEC[name] + 1, :]

    @when_first(starts)
    def _():
        gsr_out[...] = jnp.zeros_like(gsr_out)
        gemb_out[...] = jnp.zeros_like(gemb_out)
        gvec_out[...] = jnp.zeros_like(gvec_out)

    grad_pool = gpool[0][0, 0].astype(f32) + gpool[1][0, 0].astype(f32)
    for part in gpool[2:]:
        grad_pool = grad_pool + part[0].astype(f32)
    xhat, rstd = normalise(red[0])
    gvec_out[0] += fold_rows(grad_pool * xhat)
    gvec_out[1] += fold_rows(grad_pool)
    grad_red = normalise_back(grad_pool, vec("srn_g"), xhat, rstd).astype(bf16)
    gvec_out[2] += fold_rows(grad_red.astype(f32))
    gsr_out[...] += mm_tn(blk[0], grad_red)
    block_grad = mm_nt(grad_red, sr_w[...])
    for r in range(pool_rows):
        for di in range(4):
            for dj in range(4):
                k = 4 * di + dj
                start = (4 * r + di) * grid_cols + dj
                un[pl.ds(start, pool_cols, stride=4), :] = block_grad[
                    r * pool_cols : (r + 1) * pool_cols, k * C : (k + 1) * C
                ]
    grad_normed = mm_nt(gq[0], q_w[...]) + un[0:tokens, :]
    xhat0, rstd0 = normalise(emb[0])
    base = xhat0 * vec("embed_g") + vec("embed_beta")
    xhat1, rstd1 = normalise(base)
    gvec_out[3] += fold_rows(grad_normed * xhat1)
    gvec_out[4] += fold_rows(grad_normed)
    grad_base = gatt[0] + normalise_back(grad_normed, vec("norm1_g"), xhat1, rstd1)
    gvec_out[5] += fold_rows(grad_base * xhat0)
    gvec_out[6] += fold_rows(grad_base)
    grad_emb = normalise_back(grad_base, vec("embed_g"), xhat0, rstd0).astype(bf16)
    grad_emb_f = grad_emb.astype(f32)
    gvec_out[7] += fold_rows(grad_emb_f)
    gemb_out[...] += mm(grad_emb_f.T.astype(bf16), patches[0])
    pg[...] = mm_nt(grad_emb, embed_w[...])
    left = hm[0, 0]

    def row(r):
        return slice(r * grid_cols, (r + 1) * grid_cols)

    for a in (1, 2):
        side = pg[:, (3 + a) * C : (4 + a) * C] * left[grid_cols : grid_cols + tokens].astype(f32)
        total = pg[:, a * C : (a + 1) * C] + pltpu.roll(side, tokens - 1, 0)
        for r in range(grid_rows):
            gin_out[0, r, a - 1] = total[row(r)]
    rows = []
    sides = []
    for r in range(grid_rows):
        middle = pg[row(r), 0:C]
        side = pg[row(r), 3 * C : 4 * C] * left[row(r)].astype(f32)
        if r % 4 == 0:
            keep = vm[0, 2 * (r // 4)].astype(f32)
            middle = middle * keep
            side = side * keep
        rows.append(middle)
        sides.append(side)
    above = jnp.concatenate(rows, axis=0) + pltpu.roll(
        jnp.concatenate(sides, axis=0), tokens - 1, 0
    )
    grim_out[0] = above[row(0)].astype(bf16)
    for r in range(1, grid_rows):
        gin_out[0, r - 1, 1] += above[row(r)]

    @pl.when(step == pl.num_programs(0) - 1)
    def _():
        if ends:
            pack_into(
                slots, gemb_out, gvec_out, gvec_att, gqw, gkv, gsr_out, gproj, gfc1, gdw, gfc2t,
                gfc2b, own_out, other_out[0] if other_out else None, flat,
            )


def embed_back_call(
    group, feat, gpool, red, emb, gatt, gq, blk, patches, hm, vm, vecs, embed_w, q_w, sr_w,
    slots, grads, total, half,
):
    canvases = group.count
    _, grid_rows, _, grid_cols, _ = feat.shape
    tokens = grid_rows * grid_cols
    sds = jax.ShapeDtypeStruct
    return per_canvas_call(
        functools.partial(embed_back_kernel, grid_rows, grid_cols, len(gpool)),
        "embed_back",
        group,
        [Held(x, k < 2) for k, x in enumerate(gpool)] + [red, emb, gatt, gq, blk, patches, Whole(hm), Whole(vm)],
        [vecs, embed_w, q_w, sr_w, slots] + list(grads),
        [
            Whole(sds(feat.shape, f32)),
            Whole(sds((feat.shape[0], grid_cols, C), bf16)),
        ],
        [sds(half, f32), sds(half, bf16)] if half[0] > 1 else [sds(half, f32)],
        [
            pltpu.VMEM((tokens + SPARE, C), f32),
            pltpu.VMEM((tokens, KEMB), f32),
            pltpu.VMEM((16 * C, C), f32),
            pltpu.VMEM((C, KEMB), f32),
            pltpu.VMEM((8, 8, C), f32),
            pltpu.VMEM((total + SPARE, C), f32),
        ],
        flops=3e9,
    )


def add_rim_kernel(grad_in, rim_in, grad_out):
    grad_out[:, 0, 0] = grad_in[:, 0, 0] + rim_in[...].astype(f32)


def add_rim_call(grad, rim):
    canvases, grid_rows, _, grid_cols, pair_ch = grad.shape
    block = pl.BlockSpec(
        (canvases, 1, 1, grid_cols, pair_ch), lambda i: (0, grid_rows - 1, 1, 0, 0)
    )
    return pl.pallas_call(
        add_rim_kernel,
        grid=(1,),
        in_specs=[block, whole_block(rim.shape)],
        out_specs=block,
        out_shape=jax.ShapeDtypeStruct(grad.shape, f32),
        input_output_aliases={0: 0},
        name="add_rim",
    )(grad, rim)


def flat_rows():
    starts, at = {}, 0
    for name, shape in param_layout():
        starts[name] = at
        at += math.prod(shape) // C
    return starts, at


def unpack_kernel(
    slots, near, far, vecs, embed_w, q_w, kv_w, sr_w, proj_w, fc1, dwv, fc2h, flat
):
    half = near.shape[0]
    if half == 1:
        flat[0 : near.shape[1], :] = near[0].astype(f32)
    else:
        rows = (flat.shape[0] - SPARE) // (2 * half)
        first = slots[half] == 0
        for s in range(half):
            here, there = near[slots[s]][:rows], far[slots[s]][:rows]
            even, odd = 2 * s * rows, (2 * s + 1) * rows
            flat[even : even + rows, :] = jnp.where(first, here, there).astype(f32)
            flat[odd : odd + rows, :] = jnp.where(first, there, here).astype(f32)
    at, _ = flat_rows()

    def take(name, start, count):
        return flat[at[name] + start : at[name] + start + count, :]

    for i, name in enumerate(VEC_NAMES):
        vecs[i : i + 1, :] = take(name, 0, 1)
    vecs[len(VEC_NAMES) :, :] = jnp.zeros((16 - len(VEC_NAMES), C), f32)
    for a in range(3):
        embed_w[a * C : (a + 1) * C, :] = take("embed_w", a * 3 * C_IN + C_IN, C).astype(bf16)
        left = take("embed_w", a * 3 * C_IN, C_IN)
        embed_w[(3 + a) * C : (4 + a) * C, :] = jnp.concatenate(
            [jnp.zeros_like(left), left], axis=0
        ).astype(bf16)
    q_w[...] = take("q_w", 0, C).astype(bf16)
    kv_w[:, :C] = take("k_w", 0, C).astype(bf16)
    kv_w[:, C:] = take("v_w", 0, C).astype(bf16)
    sr_w[...] = take("sr_w", 0, 16 * C).astype(bf16)
    proj_w[...] = take("proj_w", 0, C).astype(bf16)
    fc2h[...] = (take("fc2_w", 0, FF) * 0.5).astype(bf16)
    dwv[...] = jnp.zeros_like(dwv)
    for c in range(FF // C):
        lanes = slice(c * C, (c + 1) * C)
        fc1[:, lanes] = flat[pl.ds(at["fc1_w"] + c, C, stride=FF // C), :].astype(bf16)
        for k in range(9):
            dwv[k : k + 1, lanes] = take("dw_w", k * (FF // C) + c, 1)
            dwv[16 + k : 17 + k, lanes] = take("fc1_b", c, 1)
        dwv[9:10, lanes] = take("dw_b", c, 1)
    dwv[25:26, :] = jnp.ones((1, FF), f32)


def unpack_call(slots, total, near, far):
    vmem_block = pl.BlockSpec(memory_space=pltpu.VMEM)
    sds = jax.ShapeDtypeStruct
    shapes = [
        sds((16, C), f32),
        sds((KEMB, C), bf16),
        sds((C, C), bf16),
        sds((C, 2 * C), bf16),
        sds((16 * C, C), bf16),
        sds((C, C), bf16),
        sds((C, FF), bf16),
        sds((32, FF), f32),
        sds((FF, C), bf16),
    ]
    return pl.pallas_call(
        unpack_kernel,
        in_specs=[pl.BlockSpec(memory_space=pltpu.SMEM), vmem_block, vmem_block],
        out_specs=[vmem_block] * len(shapes),
        out_shape=shapes,
        scratch_shapes=[pltpu.VMEM((total + SPARE, C), f32)],
        compiler_params=pltpu.CompilerParams(vmem_limit_bytes=VMEM_LIMIT),
        name="unpack",
    )(
        slots,
        pltpu.with_memory_space_constraint(near, pltpu.VMEM),
        pltpu.with_memory_space_constraint(far, pltpu.VMEM),
    )


def pack_into(
    slots, gemb, gvec_emb, gvec_att, gqw, gkv, gsr, gproj, gfc1, gdw, gfc2t, gfc2b,
    own, other, flat,
):
    at, used = flat_rows()

    def put(name, start, value):
        flat[at[name] + start : at[name] + start + value.shape[0], :] = value

    def vec_row(ref, k):
        return jnp.sum(ref[k], axis=0, keepdims=True)

    emb = gemb[...].T
    for a in range(3):
        put("embed_w", a * 3 * C_IN + C_IN, emb[a * C : (a + 1) * C])
        put("embed_w", a * 3 * C_IN, emb[(3 + a) * C + C_IN : (4 + a) * C])
    for k, name in enumerate(
        ("srn_g", "srn_b", "sr_b", "norm1_g", "norm1_b", "embed_g", "embed_beta", "embed_b")
    ):
        put(name, 0, vec_row(gvec_emb, k))
    for k, name in enumerate(("norm2_g", "norm2_b", "proj_b", "q_b", "v_b")):
        put(name, 0, vec_row(gvec_att, k))
    put("q_w", 0, gqw[...])
    put("k_w", 0, gkv[:, :C])
    put("v_w", 0, gkv[:, C:])
    put("sr_w", 0, gsr[...])
    put("proj_w", 0, gproj[...])
    put("fc2_b", 0, jnp.sum(gfc2b[...], axis=0, keepdims=True))
    put("fc2_w", 0, gfc2t[...].T)
    for c in range(FF // C):
        lanes = slice(c * C, (c + 1) * C)
        flat[pl.ds(at["fc1_w"] + c, C, stride=FF // C), :] = gfc1[:, lanes]
        for k in range(9):
            put("dw_w", k * (FF // C) + c, gdw[k : k + 1, lanes])
        put("dw_b", c, gdw[9:10, lanes])
        put("fc1_b", c, gdw[10:11, lanes])
    total = flat.shape[0] - SPARE
    flat[used:total, :] = jnp.zeros((total - used, C), f32)
    if other is None:
        own[0] = flat[0:total, :]
        return
    rows = total // (2 * own.shape[0])
    blank = jnp.zeros((own.shape[1] - rows, C), f32)
    first = slots[own.shape[0]] == 0
    for s in range(own.shape[0]):
        even = flat[2 * s * rows : (2 * s + 1) * rows, :]
        odd = flat[(2 * s + 1) * rows : (2 * s + 2) * rows, :]
        here, there = jnp.where(first, even, odd), jnp.where(first, odd, even)
        own[slots[s]] = jnp.concatenate([here, blank], axis=0)
        other[slots[s]] = jnp.concatenate([there, blank], axis=0).astype(bf16)


def other_core(block):
    size = lax.axis_size("rows")
    return lax.ppermute(block, "rows", [(i, i ^ 1) for i in range(size)])


def along_z(block, distance):
    size = lax.axis_size("rows")
    chain = size // 2
    route = [(i, 2 * ((i // 2 + distance) % chain) + i % 2) for i in range(size)]
    return lax.ppermute(block, "rows", route)


def batch_partner(index, k, size):
    return index ^ k if size & (size - 1) == 0 else (index + k) % size


def along_batch(block, k):
    size = lax.axis_size("batch")
    return lax.ppermute(block, "batch", [(i, batch_partner(i, k, size)) for i in range(size)])


def batch_source(k, size):
    return k if size & (size - 1) == 0 else (size - k) % size


def gather_chain(block):
    return jnp.stack([block] + [along_z(block, k) for k in range(1, lax.axis_size("rows") // 2)])


def z_partner(block, k):
    size = lax.axis_size("rows")
    return lax.ppermute(block, "rows", [(i, 2 * ((i // 2) ^ k) + i % 2) for i in range(size)])


def sum_over_devices(value):
    chain, batches = lax.axis_size("rows") // 2, lax.axis_size("batch")
    if chain & (chain - 1) or batches & (batches - 1):
        return lax.psum(value, ("batch", "rows"))
    value = value + other_core(value)
    for size, move in ((chain, z_partner), (batches, along_batch)):
        parts = [value] + [move(value, k) for k in range(1, size)]
        while len(parts) > 1:
            parts = [parts[i] + parts[i + 1] for i in range(0, len(parts), 2)]
        value = parts[0]
    return value


def per_step(count, wanted):
    return max(n for n in range(1, wanted + 1) if count % n == 0)


def shift_rows(block, distance):
    size = lax.axis_size("rows")
    route = [(i, i + distance) for i in range(size) if 0 <= i + distance < size]
    return lax.ppermute(block, "rows", route)


def shards(
    features,
    cotangent,
    crop_ids,
    pooled_ids,
    master_weights,
    first_moment,
    second_moment,
    weight_average,
):
    canvases, double_rows, grid_cols, pair_ch = features.shape
    grid_rows = double_rows // 2
    pool_rows, pool_cols = grid_rows // 4, grid_cols // 4
    tokens = grid_rows * grid_cols

    chain, batches = lax.axis_size("rows") // 2, lax.axis_size("batch")
    pieces = 2 * chain * batches
    part_len = master_weights.shape[0]
    total_params = part_len * pieces
    low = master_weights.astype(bf16)
    aligned = part_len % C == 0
    padded_rows = (part_len // C + 7) // 8 * 8
    if aligned:
        low = low.reshape(part_len // C, C)
        low = jnp.pad(low, ((0, padded_rows - part_len // C), (0, 0)))
    low = gather_chain(low)
    low = jnp.stack([low] + [along_batch(low, k) for k in range(1, batches)])
    row_index, batch_index = lax.axis_index("rows"), lax.axis_index("batch")
    core, z_index = row_index % 2, row_index // 2
    piece = jnp.arange(pieces, dtype=jnp.int32)
    piece_core, piece_z = piece % 2, piece // 2 % chain
    piece_batch = piece // (2 * chain)
    if batches & (batches - 1) == 0:
        batch_slot = piece_batch ^ batch_index
    else:
        batch_slot = (batch_index - piece_batch) % batches
    half_slot = batch_slot * chain + (z_index - piece_z) % chain
    slots = (piece_core ^ core) * (batches * chain) + half_slot
    pair_slots = jnp.concatenate([half_slot[::2], core[None]])
    feat = features.reshape(canvases, grid_rows, 2, grid_cols, pair_ch)
    rim = shift_rows(features[:, double_rows - 1], 1)
    above_ids = shift_rows(pooled_ids[:, pool_rows - 1], 1)
    above_ids = jnp.where(row_index == 0, -1, above_ids)
    below_ids = shift_rows(pooled_ids[:, 0], -1)
    below_ids = jnp.where(row_index == 2 * chain - 1, -1, below_ids)
    idr = jnp.concatenate(
        [
            jnp.repeat(above_ids, 4, axis=1),
            crop_ids.reshape(canvases, tokens),
            jnp.repeat(below_ids, 4, axis=1),
        ],
        axis=1,
    )
    extended = tokens + 2 * grid_cols
    idr = jnp.pad(idr, ((0, 0), (0, lane_pad(extended) - extended)), constant_values=-1)
    idr = idr[:, None]
    own_ids = pooled_ids.reshape(canvases, pool_rows * pool_cols)
    own_ids = jnp.pad(own_ids, ((0, 0), (0, C - pool_rows * pool_cols)))[:, None]

    every = Group(canvases, 0)
    hm, vm = near_masks_call(every, grid_rows, grid_cols, idr)
    low, hm, vm, own_ids, rim, pair_slots = lax.optimization_barrier(
        (low, hm, vm, own_ids, rim, pair_slots)
    )
    far_low = other_core(low)
    if aligned:
        low = low.reshape(pieces // 2, padded_rows, C)
        far_low = far_low.reshape(low.shape)
    else:
        both = jnp.stack([low, far_low]).reshape(pieces, part_len)
        low = jnp.take(both, slots, axis=0).reshape(1, total_params // C, C)
        far_low = low[:, :8]
    vecs, embed_w, q_w, kv_w, sr_w, proj_w, fc1, dwv, fc2h = unpack_call(
        pair_slots, total_params // C, low, far_low
    )

    cot = cotangent.reshape(canvases, tokens, C)
    groups = [every]
    embed_group = Group(canvases, 0, per_step(canvases, EMBED_PER))
    attend_group = Group(canvases, 0, per_step(canvases, ATTEND_PER))
    attend_back_group = Group(canvases, 0, per_step(canvases, ATTEND_BACK_PER))
    embed_back_group = Group(canvases, 0, per_step(canvases, EMBED_BACK_PER))
    embedded, chains, gathered = [], [], []
    for group in groups:
        embedded.append(embed_call(embed_group, feat, rim, hm, vm, own_ids, vecs, embed_w, q_w, sr_w))
        chains.append(gather_chain(embedded[-1][6]))
    late_idr, _ = lax.optimization_barrier((idr, embedded[-1][6]))
    token_masks = token_masks_call(every, grid_rows, grid_cols, late_idr)
    chains[-1], token_masks = lax.optimization_barrier((chains[-1], token_masks))
    q_hot, aug, aug_rows = token_masks
    gathered = [(near, other_core(near)) for near in chains]
    attended, halos = [], []
    for group, (_, base, _, q, _, _, _, _), (near, far) in zip(groups, embedded, gathered):
        attended.append(attend_call(attend_group, grid_cols, q, near, far, q_hot, base, vecs, kv_w, proj_w))
        _, _, _, _, _, head, tail = attended[-1]
        halos.append((shift_rows(tail, 1), shift_rows(head, -1)))
    layer_out, fed, back_halos = (), [], []
    for group, (_, _, _, att, sec, _, _), (top, bot) in zip(groups, attended, halos):
        wide = Group(group.count, group.first, per_step(canvases, MLP_PER))
        out = mlp_call(
            wide, sec, top, bot, hm, vm, aug, aug_rows, cot, att, fc1, dwv, fc2h, vecs, layer_out
        )
        layer_out = (out[0],)
        fed.append(out)
        back_halos.append((shift_rows(out[3], 1), shift_rows(out[2], -1)))
    backs, pool_parts = [], []
    for g, group in enumerate(groups):
        emb, _, normed, q, blk, red, _, patches = embedded[g]
        exp_scores, mix, inv, att = attended[g][:4]
        out = attend_back_call(
            attend_back_group, fed[g][1], *back_halos[g], att, cot, mix, inv, exp_scores, q, normed,
            *gathered[g], vecs, kv_w, proj_w,
        )
        backs.append(out)
        mine, theirs = out[2], other_core(out[3])
        pool_parts.append([mine, theirs])
        for k in range(1, chain):
            both = mine[k].astype(f32) + theirs[k].astype(f32)
            pool_parts[-1].append(along_z(both.astype(bf16), -k))
    emb, _, _, _, blk, red, _, patches = embedded[0]
    gatt, gq, _, _, g_proj_w, g_kv_w, g_q_w, gvec_att = backs[0]
    half = (pieces // 2, padded_rows, C) if aligned else (1, total_params // C, C)
    g_in, grim, own, *other = embed_back_call(
        embed_back_group, feat, pool_parts[0], red, emb, gatt, gq, blk, patches, hm, vm,
        vecs, embed_w, q_w, sr_w,
        pair_slots, [gvec_att, g_q_w, g_kv_w, g_proj_w, *fed[0][4:]], total_params // C, half,
    )
    layer_out = layer_out[0]
    input_grad = add_rim_call(g_in, shift_rows(grim, -1))

    if aligned:
        own = own.reshape(batches, chain, padded_rows, C)
        other = other[0].reshape(batches, chain, padded_rows, C)
    else:
        order = jnp.zeros((pieces,), jnp.int32).at[slots].set(piece)
        both = jnp.take(own.reshape(pieces, part_len), order, axis=0)
        both = both.reshape(2, batches, chain, part_len)
        own, other = both[0], both[1].astype(bf16)
    own = own + other_core(other).astype(f32)
    own = sum(
        [
            along_batch(own[batch_source(k, batches)].astype(bf16), k).astype(f32)
            for k in range(1, batches)
        ],
        own[0],
    )
    own, input_grad = lax.optimization_barrier((own, input_grad))
    input_grad = input_grad.reshape(features.shape)
    shard_grad = sum(
        [along_z(own[k].astype(bf16), -k).astype(f32) for k in range(1, chain)], own[0]
    )
    if aligned:
        squares = jnp.sum((shard_grad * shard_grad).reshape(-1, 8, C), axis=0)
    else:
        squares = jnp.broadcast_to(jnp.sum(shard_grad * shard_grad) / (8 * C), (8, C))
    square_sum = jnp.sum(sum_over_devices(squares))
    if aligned:
        shard_grad = shard_grad[: part_len // C]
    shard_grad = shard_grad.reshape(part_len)
    grad_norm = jnp.sqrt(square_sum)
    clip_limit = math.sqrt(total_params)
    clipped = shard_grad * (clip_limit / jnp.maximum(grad_norm, clip_limit))
    new_first = BETA_ONE * first_moment + (1.0 - BETA_ONE) * clipped
    new_second = BETA_TWO * second_moment + (1.0 - BETA_TWO) * clipped * clipped
    first_hat = new_first / (1.0 - BETA_ONE**UPDATES)
    second_hat = new_second / (1.0 - BETA_TWO**UPDATES)
    new_weights = master_weights * (1.0 - LEARN_RATE * DECAY_RATE) - LEARN_RATE * first_hat / (
        jnp.sqrt(second_hat) + ADAM_EPS
    )
    new_average = AVERAGE_KEEP * weight_average + (1.0 - AVERAGE_KEEP) * new_weights
    layer_out = layer_out.reshape(cotangent.shape)
    return (layer_out, input_grad, grad_norm, new_first, new_second, new_weights, new_average)


def solution(mesh):
    placed = (
        P("batch", "rows", None, None),
        P("batch", "rows", None, None),
        P("batch", "rows", None),
        P("batch", "rows", None),
        P(("batch", "rows")),
        P(("batch", "rows")),
        P(("batch", "rows")),
        P(("batch", "rows")),
    )
    return jax.shard_map(
        shards,
        mesh=mesh,
        in_specs=placed,
        out_specs=(
            P("batch", "rows", None, None),
            P("batch", "rows", None, None),
            P(),
            P(("batch", "rows")),
            P(("batch", "rows")),
            P(("batch", "rows")),
            P(("batch", "rows")),
        ),
        check_vma=False,
    )
```

```python
import functools
import math

import jax
import jax.numpy as jnp
from jax import lax
from jax.experimental import pallas as pl
from jax.experimental.pallas import tpu as pltpu
from jax.sharding import PartitionSpec as P

C_IN = 64
C = 128
HEADS = 2
FF = 1024
HEAD_DIM = 64
UPDATES = 10

NORM_EPS = 1e-06
BETA_ONE = 0.9
BETA_TWO = 0.999
LEARN_RATE = 0.1
DECAY_RATE = 0.05
ADAM_EPS = 1e-08
AVERAGE_KEEP = 0.9
MASKED = -1e30
ROOT_HALF = 0.7071067811865476
LOG2E = 1.4426950408889634
PDF_SHIFT = math.log2(2.0 / math.sqrt(math.pi))
KEMB = 6 * C
K3 = 3 * C

f32 = jnp.float32
bf16 = jnp.bfloat16
VMEM_LIMIT = 60 * 2**20
SPARE = 32
MLP_PER = 1
EMBED_PER = 1
ATTEND_PER = 1
ATTEND_BACK_PER = 1
EMBED_BACK_PER = 1

VEC_NAMES = (
    "embed_b", "embed_g", "embed_beta", "norm1_g", "norm1_b", "q_b", "v_b", "sr_b",
    "srn_g", "srn_b", "proj_b", "norm2_g", "norm2_b", "fc2_b",
)
VEC = {name: i for i, name in enumerate(VEC_NAMES)}


def param_layout():
    return [
        ("embed_w", (9 * C_IN, C)),
        ("embed_b", (C,)),
        ("embed_g", (C,)),
        ("embed_beta", (C,)),
        ("norm1_g", (C,)),
        ("norm1_b", (C,)),
        ("q_w", (C, C)),
        ("q_b", (C,)),
        ("k_w", (C, C)),
        ("v_w", (C, C)),
        ("v_b", (C,)),
        ("sr_w", (16 * C, C)),
        ("sr_b", (C,)),
        ("srn_g", (C,)),
        ("srn_b", (C,)),
        ("proj_w", (C, C)),
        ("proj_b", (C,)),
        ("norm2_g", (C,)),
        ("norm2_b", (C,)),
        ("fc1_w", (C, FF)),
        ("fc1_b", (FF,)),
        ("dw_w", (9, FF)),
        ("dw_b", (FF,)),
        ("fc2_w", (FF, C)),
        ("fc2_b", (C,)),
    ]


def mm(left, right):
    return jnp.dot(left, right, preferred_element_type=f32)


def mm_nt(left, right):
    return lax.dot_general(
        left, right, (((1,), (1,)), ((), ())), preferred_element_type=f32
    )


def mm_tn(left, right):
    return lax.dot_general(
        left, right, (((0,), (0,)), ((), ())), preferred_element_type=f32
    )


def split_hi_lo(value):
    high = value.astype(bf16)
    return high, (value - high.astype(f32)).astype(bf16)


def normalise(value):
    centre = value - jnp.mean(value, axis=-1, keepdims=True)
    rstd = lax.rsqrt(jnp.mean(centre * centre, axis=-1, keepdims=True) + NORM_EPS)
    return centre * rstd, rstd


def normalise_back(grad, gain, xhat, rstd):
    scaled = grad * gain
    first = jnp.mean(scaled, axis=-1, keepdims=True)
    other = jnp.mean(scaled * xhat, axis=-1, keepdims=True)
    return rstd * (scaled - first - xhat * other)


def fold_rows(value):
    return jnp.sum(value.reshape(value.shape[0] // 8, 8, value.shape[1]), axis=0)


def lane_pad(count):
    return (count + C - 1) // C * C


def crop_columns(idr, grid_cols):
    ids = jnp.broadcast_to(idr[0], (8, idr.shape[2]))
    width = ids.shape[1]
    column = lax.broadcasted_iota(jnp.int32, ids.shape, 1) % grid_cols
    kind = lax.broadcasted_iota(jnp.int32, ids.shape, 0)
    left = (ids == pltpu.roll(ids, 1, 1)) & (column != 0)
    right = (ids == pltpu.roll(ids, width - 1, 1)) & (column != grid_cols - 1)
    upper = ids == pltpu.roll(ids, grid_cols, 1)
    lower = ids == pltpu.roll(ids, width - grid_cols, 1)
    rows = jnp.zeros(ids.shape, f32)
    for k, same in enumerate((left, right, upper, lower)):
        rows = jnp.where((kind == k) & same, 1.0, rows)
    return rows.T


def spread(columns, k, start, count):
    return jnp.broadcast_to(columns[start : start + count, k : k + 1], (count, C))


def tap_rows(idr, grid_cols):
    ids = jnp.broadcast_to(idr[0], (32, idr.shape[2]))
    width = ids.shape[1]
    column = lax.broadcasted_iota(jnp.int32, ids.shape, 1) % grid_cols
    kind = lax.broadcasted_iota(jnp.int32, ids.shape, 0) % 16
    rows = jnp.where(kind == 9, 1.0, jnp.zeros(ids.shape, f32))
    for a in (-1, 0, 1):
        for b in (-1, 0, 1):
            k = 3 * (a + 1) + b + 1
            away = (-(a * grid_cols + b)) % width
            same = ids == (pltpu.roll(ids, away, 1) if away else ids)
            inside = (column + b >= 0) & (column + b < grid_cols)
            rows = jnp.where((kind == k) & same & inside, 1.0, rows)
    return pltpu.roll(rows, width - grid_cols, 1)


def one_hot_digits(low, high):
    lane = lax.broadcasted_iota(jnp.int32, (low.shape[0], C), 1).astype(f32)
    return (lane == low) | (lane == high + 32.0)


def when_first(starts):
    def run(body):
        if starts:
            pl.when(pl.program_id(0) == 0)(body)

    return run


class Stack:
    def __init__(self, value):
        self.value = value
        self.shape = value.shape


class Whole:
    def __init__(self, value):
        self.value = value
        self.shape = value.shape


class Held:
    def __init__(self, value, behind=False):
        self.value, self.behind = value, behind
        self.shape = value.shape


class Group:
    def __init__(self, count, first, per=1):
        self.count, self.first, self.per = count, first, per


def canvas_block(array, group):
    shape, per = array.shape, group.per
    at = group.first // per if isinstance(array, Whole) else 0
    if isinstance(array, Held):
        return pl.BlockSpec(memory_space=pltpu.VMEM)
    if isinstance(array, Stack):
        return pl.BlockSpec((shape[0], per) + shape[2:], lambda i: (0, i) + (0,) * (len(shape) - 2))
    return pl.BlockSpec((per,) + shape[1:], lambda i: (i + at,) + (0,) * (len(shape) - 1))


def bare(array):
    return array.value if isinstance(array, (Stack, Whole, Held)) else array


def whole_block(shape):
    return pl.BlockSpec(shape, lambda i: (0,) * len(shape))


def per_canvas_call(
    kernel, name, group, canvas_in, shared_in, canvas_out, shared_out, scratch, flops=0, earlier=(),
    inside=False,
):
    steps = group.count // group.per
    inputs = [
        pltpu.with_memory_space_constraint(x.value, pltpu.VMEM) if isinstance(x, Held) else bare(x)
        for x in canvas_in
    ] + list(shared_in)
    outputs = [bare(x) for x in canvas_out] + list(shared_out)
    in_specs = [canvas_block(x, group) for x in canvas_in]
    in_specs += [
        pl.BlockSpec(memory_space=pltpu.SMEM) if x.ndim == 1 else whole_block(x.shape)
        for x in shared_in
    ]
    aliases = {}
    if earlier:
        aliases = {len(inputs) + k: place for k, (place, _) in enumerate(earlier)}
        skip = slice(len(inputs), len(inputs) + len(earlier))
        in_specs += [pl.BlockSpec(memory_space=pl.ANY)] * len(earlier)
        inputs += [array for _, array in earlier]

    else:
        skip = slice(len(inputs), len(inputs))

    def body(*refs):
        refs = list(refs[: skip.start] + refs[skip.stop :])
        out_at = len(canvas_in) + len(shared_in)
        per_canvas = list(enumerate(canvas_in)) + [
            (out_at + k, x) for k, x in enumerate(canvas_out)
        ]
        if inside:
            views = list(refs)
            for k, x in per_canvas:
                if isinstance(x, Held):
                    views[k] = refs[k].at[pl.ds(pl.program_id(0) * group.per, group.per)]
            kernel(*views)
            return
        for p in range(group.per):
            views = list(refs)
            for k, x in per_canvas:
                behind = isinstance(x, Stack) or (isinstance(x, Held) and x.behind)
                at = pl.ds(pl.program_id(0) * group.per + p, 1) if isinstance(x, Held) else pl.ds(p, 1)
                views[k] = refs[k].at[:, at] if behind else refs[k].at[at]
            kernel(p == 0, p == group.per - 1, *views)

    bytes_moved = sum(x.size * x.dtype.itemsize for x in inputs) + sum(
        math.prod(x.shape) * x.dtype.itemsize for x in outputs
    )
    return pl.pallas_call(
        body,
        grid=(steps,),
        in_specs=in_specs,
        out_specs=[canvas_block(x, group) for x in canvas_out]
        + [whole_block(x.shape) for x in shared_out],
        out_shape=outputs,
        scratch_shapes=scratch,
        input_output_aliases=aliases,
        compiler_params=pltpu.CompilerParams(vmem_limit_bytes=VMEM_LIMIT),
        cost_estimate=pl.CostEstimate(
            flops=int(flops * group.count), bytes_accessed=int(bytes_moved), transcendentals=0
        ),
        name=name,
    )(*inputs)


def near_masks_kernel(grid_rows, grid_cols, starts, ends, idr, hm_out, vm_out):
    columns = crop_columns(idr, grid_cols)
    extended = (grid_rows + 2) * grid_cols
    for k in range(2):
        hm_out[0, k] = spread(columns, k, 0, extended).astype(bf16)
    for r in range(0, grid_rows, 4):
        k = 2 * (r // 4)
        vm_out[0, k] = spread(columns, 2, (r + 1) * grid_cols, grid_cols).astype(bf16)
        vm_out[0, k + 1] = spread(columns, 3, (r + 4) * grid_cols, grid_cols).astype(bf16)


def near_masks_call(group, grid_rows, grid_cols, idr):
    canvases = idr.shape[0]
    sds = jax.ShapeDtypeStruct
    return per_canvas_call(
        functools.partial(near_masks_kernel, grid_rows, grid_cols),
        "near_masks",
        group,
        [idr],
        [],
        [
            sds((canvases, 2, (grid_rows + 2) * grid_cols, C), bf16),
            sds((canvases, grid_rows // 2, grid_cols, C), bf16),
        ],
        [],
        [],
    )


def token_masks_kernel(grid_cols, starts, ends, idr, hot_out, aug_out, row_out):
    tokens = hot_out.shape[1]
    ids = jnp.broadcast_to(idr[0], (8, idr.shape[2]))
    kind = lax.broadcasted_iota(jnp.int32, ids.shape, 0)
    column = jnp.where(kind == 0, ids % 32, ids // 32).astype(f32).T
    column = column[grid_cols : grid_cols + tokens]
    hot = one_hot_digits(column[:, 0:1], column[:, 1:2])
    hot_out[0] = jnp.where(hot, 1.0, 0.0).astype(bf16)
    taps = tap_rows(idr, grid_cols)
    for q in range(2):
        rows = [taps[:, r * grid_cols : (r + 1) * grid_cols] for r in range(q, tokens // grid_cols, 2)]
        row_out[0, q] = jnp.concatenate(rows, axis=1).astype(bf16)
    aug_out[0, :, 0:32] = taps.T[:tokens].astype(bf16)
    aug_out[0, :, 32:] = jnp.zeros((tokens, C - 32), bf16)


def token_masks_call(group, grid_rows, grid_cols, idr):
    canvases, tokens = idr.shape[0], grid_rows * grid_cols
    sds = jax.ShapeDtypeStruct
    return per_canvas_call(
        functools.partial(token_masks_kernel, grid_cols),
        "token_masks",
        group,
        [idr],
        [],
        [
            sds((canvases, tokens, C), bf16),
            sds((canvases, tokens, C), bf16),
            sds((canvases, 2, 32, tokens // 2), bf16),
        ],
        [],
        [],
    )


def fill_patches(grid_rows, grid_cols, feat, rim, hm, vm, patches):
    tokens = grid_rows * grid_cols
    left = hm[0, 0]
    for a in range(3):
        rows = []
        for r in range(grid_rows):
            if a == 0:
                rows.append(rim[0] if r == 0 else feat[0, r - 1, 1])
            else:
                rows.append(feat[0, r, a - 1])
        source = jnp.concatenate(rows, axis=0)
        rolled = pltpu.roll(source.astype(f32), 1, 0)
        mask_at = 0 if a == 0 else grid_cols
        shifted = (rolled * left[mask_at : mask_at + tokens].astype(f32)).astype(bf16)
        if a == 0:
            for r in range(grid_rows):
                here = slice(r * grid_cols, (r + 1) * grid_cols)
                if r % 4 == 0:
                    keep = vm[0, 2 * (r // 4)]
                    patches[here, 0:C] = source[here] * keep
                    patches[here, 3 * C : 4 * C] = shifted[here] * keep
                else:
                    patches[here, 0:C] = source[here]
                    patches[here, 3 * C : 4 * C] = shifted[here]
        else:
            patches[:, a * C : (a + 1) * C] = source
            patches[:, (3 + a) * C : (4 + a) * C] = shifted


def embed_kernel(
    grid_rows, grid_cols, starts, ends,
    feat, rim, hm, vm, own_ids, vecs, embed_w, q_w, sr_w,
    emb_out, base_out, norm_out, q_out, blk_out, red_out, pool_out, patch_out,
    tok, blkf,
):
    pool_rows, pool_cols = grid_rows // 4, grid_cols // 4
    patches = patch_out.at[0]
    fill_patches(grid_rows, grid_cols, feat, rim, hm, vm, patches)
    vec = lambda name: vecs[VEC[name] : VEC[name] + 1, :]
    embedded = mm(patches[...], embed_w[...]) + vec("embed_b")
    emb_out[0] = embedded
    base = normalise(embedded)[0] * vec("embed_g") + vec("embed_beta")
    base_out[0] = base
    normed = (normalise(base)[0] * vec("norm1_g") + vec("norm1_b")).astype(bf16)
    norm_out[0] = normed
    queries = (mm(normed, q_w[...]) + vec("q_b")).astype(bf16)
    q_out[0] = queries * bf16(HEAD_DIM ** (-0.5))
    tok[0 : normed.shape[0], :] = normed.astype(f32)
    for r in range(pool_rows):
        for di in range(4):
            for dj in range(4):
                k = 4 * di + dj
                start = (4 * r + di) * grid_cols + dj
                blkf[r * pool_cols : (r + 1) * pool_cols, k * C : (k + 1) * C] = tok[
                    pl.ds(start, pool_cols, stride=4), :
                ]
    blocks = blkf[0 : pool_rows * pool_cols, :].astype(bf16)
    blk_out[0] = blocks
    reduced = mm(blocks, sr_w[...]) + vec("sr_b")
    red_out[0] = reduced
    own = pool_rows * pool_cols
    pooled = normalise(reduced)[0] * vec("srn_g") + vec("srn_b")
    ids = jnp.broadcast_to(own_ids[0], (8, C))
    kind = lax.broadcasted_iota(jnp.int32, ids.shape, 0)
    digits = jnp.where(kind == 0, ids % 32, jnp.where(kind == 1, ids // 32, 0)).astype(f32)
    pool_out[0] = jnp.concatenate([pooled, digits], axis=0).astype(bf16)


def embed_call(group, feat, rim, hm, vm, own_ids, vecs, embed_w, q_w, sr_w):
    canvases = group.count
    _, grid_rows, _, grid_cols, _ = feat.shape
    tokens = grid_rows * grid_cols
    own = tokens // 16
    sds = jax.ShapeDtypeStruct
    return per_canvas_call(
        functools.partial(embed_kernel, grid_rows, grid_cols),
        "embed",
        group,
        [Whole(feat), Held(rim), Whole(hm), Whole(vm), Whole(own_ids)],
        [vecs, embed_w, q_w, sr_w],
        [
            sds((canvases, tokens, C), f32),
            sds((canvases, tokens, C), f32),
            sds((canvases, tokens, C), bf16),
            sds((canvases, tokens, C), bf16),
            sds((canvases, own, 16 * C), bf16),
            sds((canvases, own, C), f32),
            sds((canvases, own + 8, C), bf16),
            sds((canvases, tokens, KEMB), bf16),
        ],
        [],
        [
            pltpu.VMEM((tokens + SPARE, C), f32),
            pltpu.VMEM((own + 8, 16 * C), f32),
        ],
        flops=2e9,
    )


def keys_values(pooled, kv_w, vecs):
    both = mm(pooled, kv_w)
    keys = both[:, :C].astype(bf16)
    values = (both[:, C:] + vecs[VEC["v_b"] : VEC["v_b"] + 1, :]).astype(bf16)
    return keys, values


def head_lanes(shape, head):
    lane = lax.broadcasted_iota(jnp.int32, shape, 1)
    return (lane // HEAD_DIM) == head


def all_pooled_rows(near, far):
    own = near.shape[2] - 8
    parts = [ref[k, 0].astype(f32) for ref in (near, far) for k in range(ref.shape[0])]
    return jnp.concatenate([part[:own] for part in parts], axis=0), [p[own:] for p in parts]


def attend_kernel(
    starts, ends,
    q, near, far, q_hot, base, vecs, kv_w, proj_w,
    exp_out, mix_out, inv_out, att_out, sec_out, head_out, tail_out,
):
    vec = lambda name: vecs[VEC[name] : VEC[name] + 1, :]
    pooled, digits = all_pooled_rows(near, far)
    keys, values = keys_values(pooled.astype(bf16), kv_w[...], vecs)
    values_t = values.astype(f32).T.astype(bf16)
    tokens = q.shape[1]
    own = near.shape[2] - 8
    columns = jnp.concatenate(digits, axis=0).T
    hot = [
        one_hot_digits(columns[:own, 8 * k : 8 * k + 1], columns[:own, 8 * k + 1 : 8 * k + 2])
        for k in range(len(digits))
    ]
    k_hot = jnp.where(jnp.concatenate(hot, axis=0), 0.0, MASKED).astype(bf16)
    q_cat = jnp.concatenate([q[0], q_hot[0]], axis=1)
    for h in range(HEADS):
        k_own = jnp.where(head_lanes(keys.shape, h), keys, jnp.zeros_like(keys))
        scores = mm_nt(jnp.concatenate([k_own, k_hot], axis=1), q_cat)
        peak = jnp.max(scores, axis=0, keepdims=True)
        raised = jnp.exp(scores - peak)
        inverse = 1.0 / jnp.sum(raised, axis=0, keepdims=True)
        low = raised.astype(bf16)
        exp_out[0, h] = low
        inv_out[0, 4 * h : 4 * h + 4, :] = jnp.broadcast_to(inverse, (4, tokens))
        part = slice(h * HEAD_DIM, (h + 1) * HEAD_DIM)
        mix_out[0, part, :] = mm(values_t[part], low) * inverse
    mixed = mix_out[0].T.astype(bf16)
    attended = base[0] + mm(mixed, proj_w[...]) + vec("proj_b")
    att_out[0] = attended
    second = (normalise(attended)[0] * vec("norm2_g") + vec("norm2_b")).astype(bf16)
    sec_out[0] = second
    grid_cols = head_out.shape[1]
    head_out[0] = second[:grid_cols]
    tail_out[0] = second[tokens - grid_cols :]


def attend_call(group, grid_cols, q, near, far, q_hot, base, vecs, kv_w, proj_w):
    canvases, tokens, _ = q.shape
    total = 2 * near.shape[0] * (near.shape[2] - 8)
    sds = jax.ShapeDtypeStruct
    return per_canvas_call(
        attend_kernel,
        "attend",
        group,
        [q, Held(near, True), Held(far, True), Whole(q_hot), base],
        [vecs, kv_w, proj_w],
        [
            sds((canvases, HEADS, total, tokens), bf16),
            sds((canvases, C, tokens), f32),
            sds((canvases, 8, tokens), f32),
            sds((canvases, tokens, C), f32),
            sds((canvases, tokens, C), bf16),
            sds((canvases, grid_cols, C), bf16),
            sds((canvases, grid_cols, C), bf16),
        ],
        [],
        [],
        flops=2.5e9,
    )


def attend_back_kernel(
    grid_cols, starts, ends,
    gsec, gtop, gbot, att, cot, mix, inv, exp_in, q, normed, near, far, vecs, kv_w, proj_w,
    gatt_out, gq_out, gnear_out, gfar_out, gproj_out, gkv_out, gqw_out, gvec_out,
):
    step = pl.program_id(0)
    vec = lambda name: vecs[VEC[name] : VEC[name] + 1, :]

    @when_first(starts)
    def _():
        gproj_out[...] = jnp.zeros_like(gproj_out)
        gkv_out[...] = jnp.zeros_like(gkv_out)
        gqw_out[...] = jnp.zeros_like(gqw_out)
        gvec_out[...] = jnp.zeros_like(gvec_out)

    tokens = q.shape[1]
    last = tokens - grid_cols
    grad_second = jnp.concatenate(
        [
            gsec[0, :grid_cols] + gtop[0].astype(f32),
            gsec[0, grid_cols:last],
            gsec[0, last:] + gbot[0].astype(f32),
        ],
        axis=0,
    )
    xhat, rstd = normalise(att[0])
    gvec_out[0] += fold_rows(grad_second * xhat)
    gvec_out[1] += fold_rows(grad_second)
    grad_att = cot[0].astype(f32) + normalise_back(grad_second, vec("norm2_g"), xhat, rstd)
    gatt_out[0] = grad_att
    branch = grad_att.astype(bf16)
    gvec_out[2] += fold_rows(branch.astype(f32))
    mixed_t = mix[0]
    gproj_out[...] += mm(mixed_t.astype(bf16), branch)
    grad_mix_t = mm_nt(proj_w[...], branch)
    inverses = inv[0]
    pooled_f, _ = all_pooled_rows(near, far)
    keys, values = keys_values(pooled_f.astype(bf16), kv_w[...], vecs)
    keys_t = keys.astype(f32).T.astype(bf16)
    gq_parts = []
    gk_parts = []
    gv_parts = []
    for h in range(HEADS):
        part = slice(h * HEAD_DIM, (h + 1) * HEAD_DIM)
        scaled = (grad_mix_t[part] * inverses[4 * h : 4 * h + 1]).astype(bf16)
        middle = jnp.sum(scaled.astype(f32) * mixed_t[part], axis=0, keepdims=True)
        raised = exp_in[0, h]
        pair = jnp.concatenate([scaled, scaled], axis=0)
        gv_parts.append(mm_nt(raised, pair))
        v_own = jnp.where(head_lanes(values.shape, h), values, jnp.zeros_like(values))
        grad_p = mm(v_own, pair)
        grad_s = (raised.astype(f32) * (grad_p - middle)).astype(bf16)
        gq_parts.append(mm(keys_t[part], grad_s))
        gk_parts.append(mm(grad_s, q[0]))
    first = head_lanes(gk_parts[0].shape, 0)
    grad_keys = jnp.where(first, gk_parts[0], gk_parts[1])
    grad_values = jnp.where(first, gv_parts[0], gv_parts[1])
    grad_q = (jnp.concatenate(gq_parts, axis=0) * HEAD_DIM ** (-0.5)).T.astype(bf16)
    gq_out[0] = grad_q
    gvec_out[3] += fold_rows(grad_q.astype(f32))
    gvec_out[4] += fold_rows(grad_values)
    gqw_out[...] += mm_tn(normed[0], grad_q)
    k_high, k_low = split_hi_lo(grad_keys)
    v_high, v_low = split_hi_lo(grad_values)
    high = jnp.concatenate([k_high, v_high], axis=1)
    low = jnp.concatenate([k_low, v_low], axis=1)
    pooled_t = pooled_f.T.astype(bf16)
    gkv_out[...] += mm(pooled_t, high) + mm(pooled_t, low)
    grad_pool = mm_nt(high, kv_w[...]) + mm_nt(low, kv_w[...])
    chain, own = near.shape[0], near.shape[2] - 8
    for k in range(chain):
        gnear_out[k, 0] = grad_pool[k * own : (k + 1) * own].astype(bf16)
        gfar_out[k, 0] = grad_pool[(chain + k) * own : (chain + k + 1) * own].astype(bf16)


def attend_back_call(
    group, gsec, gtop, gbot, att, cot, mix, inv, exp_in, q, normed, near, far, vecs, kv_w, proj_w
):
    canvases, tokens, _ = q.shape
    sds = jax.ShapeDtypeStruct
    gpool = sds((near.shape[0], canvases, near.shape[2] - 8, C), bf16)
    return per_canvas_call(
        functools.partial(attend_back_kernel, gtop.shape[1]),
        "attend_back",
        group,
        [
            gsec, Held(gtop), Held(gbot), att, Whole(cot), mix, inv, exp_in, q, normed,
            Held(near, True), Held(far, True),
        ],
        [vecs, kv_w, proj_w],
        [
            sds((canvases, tokens, C), f32),
            sds((canvases, tokens, C), bf16),
            Stack(gpool),
            Stack(gpool),
        ],
        [
            sds((C, C), f32),
            sds((C, 2 * C), f32),
            sds((C, C), f32),
            sds((5, 8, C), f32),
        ],
        [],
        flops=3.5e9,
    )


def mlp_kernel(
    grid_rows, grid_cols,
    sec, top, bot, hm, vm, aug, aug_rows, cot, att, fc1, dwv, fc2h, vecs,
    lo, gsec, gtop, gbot, gfc1, gdw, gfc2t, gfc2b,
    wf, wt, f2t, xf, xt, acc, ones_grad, act, gm, gx,
):
    tokens = grid_rows * grid_cols
    half = tokens // 2
    pairs = grid_rows // 2
    extended = tokens + 2 * grid_cols
    step = pl.program_id(0)
    per = sec.shape[0]

    @pl.when(step == 0)
    def _():
        first = fc1[...].astype(f32)
        for b in range(3):
            rows = [first * (dwv[3 * a + b : 3 * a + b + 1, :] * ROOT_HALF) for a in range(3)]
            ends = (rows[0] + rows[2]) * 0.5
            mixed = [rows[0], ends + rows[1] * 0.5, ends - rows[1] * 0.5, rows[2]]
            for k in range(4):
                wf[k, b * C : (b + 1) * C, :] = mixed[k].astype(bf16)
        high, low = split_hi_lo(dwv[0:16, :] * dwv[16:32, :] * ROOT_HALF)
        for k in (0, 3):
            wf[k, K3 : K3 + 16, :] = high
            wf[k, K3 + 16 : K3 + 32, :] = low
            wf[k, K3 + 32 :, :] = jnp.zeros((C - 32, FF), bf16)
        for k in range(4):
            wt[k] = wf[k, :K3, :].T
        f2t[...] = fc2h[...].T
        acc[...] = jnp.zeros_like(acc)
        ones_grad[...] = jnp.zeros_like(ones_grad)
        gfc2t[...] = jnp.zeros_like(gfc2t)
        gfc2b[...] = jnp.zeros_like(gfc2b)

    def row(r):
        return slice(r * grid_cols, (r + 1) * grid_cols)

    def upper(r, p):
        return vm[p, 2 * (r // 4)].astype(f32) if r % 4 == 0 else None

    def lower(r, p):
        return vm[p, 2 * (r // 4) + 1].astype(f32) if r % 4 == 3 else None

    def kept(value, mask):
        return value if mask is None else value * mask

    for p in range(per):
        wide = jnp.concatenate(
            [top[p].astype(f32), sec[p].astype(f32), bot[p].astype(f32)], axis=0
        )
        for b in range(3):
            moved = wide
            if b != 1:
                moved = pltpu.roll(wide, 1 if b == 0 else extended - 1, 0)
                moved = moved * hm[p, b // 2].astype(f32)
            for i in range(pairs):
                d0, d1, d2, d3 = [moved[row(2 * i + k)] for k in range(4)]
                d0, d3 = kept(d0, upper(2 * i, p)), kept(d3, lower(2 * i + 1, p))
                at = slice(p * half + i * grid_cols, p * half + (i + 1) * grid_cols)
                for k, value in enumerate((d0 - d2, d1 + d2, d2 - d1, d1 - d3)):
                    xf[k, at, b * C : (b + 1) * C] = value.astype(bf16)
        mine = slice(p * half, (p + 1) * half)
        for k in range(4):
            xt[k, :, mine] = xf[k, mine, :K3].T
        for i in range(pairs):
            at = slice(p * half + i * grid_cols, p * half + (i + 1) * grid_cols)
            xf[0, at, K3:] = aug[p, row(2 * i)]
            xf[3, at, K3:] = -aug[p, row(2 * i + 1)]

    def by_parity(ref):
        return jnp.concatenate(
            [ref[p, row(2 * i + q)] for q in range(2) for p in range(per) for i in range(pairs)],
            axis=0,
        )

    given = by_parity(cot)
    m0 = mm(xf[0], wf[0])
    m1 = mm(xf[1, :, :K3], wf[1, :K3])
    m2 = mm(xf[2, :, :K3], wf[2, :K3])
    m3 = mm(xf[3], wf[3])
    d = mm(given, f2t[...])
    grads = []
    for q, u in enumerate((m0 + (m1 + m2), (m1 - m2) - m3)):
        at = slice(q * per * half, (q + 1) * per * half)
        phi = 1.0 + lax.erf(u)
        act[at, :] = (u * phi).astype(bf16)
        pdf = jnp.exp2(PDF_SHIFT - u * u * LOG2E)
        grads.append((phi + u * pdf) * d[at])
    even, odd = grads
    for k, value in enumerate((even, even + odd, even - odd, -odd)):
        gm[k] = value.astype(bf16)
    for k in range(4):
        acc[k] += mm(xt[k], gm[k])
        gx[k] = mm(gm[k], wt[k])
    for q in range(2):
        taps = jnp.concatenate([aug_rows[p, q] for p in range(per)], axis=1)
        ones_grad[...] += mm(taps, gm[3 * q] if q == 0 else -gm[3])
    given_f = given.astype(f32)
    gfc2t[...] += mm(given_f.T.astype(bf16), act[...])
    gfc2b[...] += fold_rows(given_f)
    mlp_out = mm(act[...], fc2h[...]) * (2 * ROOT_HALF) + vecs[VEC["fc2_b"] : VEC["fc2_b"] + 1, :]
    for p in range(per):
        total = None
        for b in range(3):
            rows = [None] * (grid_rows + 2)
            lanes = slice(b * C, (b + 1) * C)
            for i in range(pairs):
                at = slice(p * half + i * grid_cols, p * half + (i + 1) * grid_cols)
                c0, c1, c2, c3 = [gx[k, at, lanes] for k in range(4)]
                d0, d3 = kept(c0, upper(2 * i, p)), kept(-c3, lower(2 * i + 1, p))
                for k, value in enumerate((d0, (c1 - c2) + c3, (c1 + c2) - c0, d3)):
                    e = 2 * i + k
                    rows[e] = value if rows[e] is None else rows[e] + value
            side = jnp.concatenate(rows, axis=0)
            if b != 1:
                side = pltpu.roll(
                    side * hm[p, b // 2].astype(f32), extended - 1 if b == 0 else 1, 0
                )
            total = side if total is None else total + side
        total = total * (2 * ROOT_HALF)
        gtop[p] = total[0:grid_cols].astype(bf16)
        gsec[p] = total[grid_cols : grid_cols + tokens]
        gbot[p] = total[grid_cols + tokens :].astype(bf16)
        for i in range(pairs):
            for q in range(2):
                at = (q * per + p) * half + i * grid_cols
                r = row(2 * i + q)
                lo[p, r] = (att[p, r] + mlp_out[at : at + grid_cols]).astype(bf16)

    @pl.when(step == pl.num_programs(0) - 1)
    def _():
        first = fc1[...].astype(f32)
        summed = None
        bias = ones_grad[0:16, :]
        for b in range(3):
            lanes = slice(b * C, (b + 1) * C)
            both = (acc[1, lanes, :] + acc[2, lanes, :]) * 0.5
            apart = (acc[1, lanes, :] - acc[2, lanes, :]) * 0.5
            for a, tap in enumerate((acc[0, lanes, :] + both, apart, acc[3, lanes, :] + both)):
                k = 3 * a + b
                term = tap * dwv[k : k + 1, :]
                summed = term if summed is None else summed + term
                gdw[k : k + 1, :] = (
                    jnp.sum(tap * first, axis=0, keepdims=True) + bias[k : k + 1] * dwv[16:17, :]
                )
        gfc1[...] = summed
        gdw[9:10, :] = bias[9:10]
        gdw[10:11, :] = jnp.sum(bias[0:9] * dwv[0:9, :], axis=0, keepdims=True)
        gdw[11:16, :] = jnp.zeros((5, FF), f32)
        gfc2t[...] = gfc2t[...] * ROOT_HALF


def mlp_call(
    group, sec, top, bot, hm, vm, aug, aug_rows, cot, att, fc1, dwv, fc2h, vecs, earlier
):
    canvases, tokens, _ = sec.shape
    grid_cols = top.shape[1]
    grid_rows = tokens // grid_cols
    stacked = group.per * tokens
    sds = jax.ShapeDtypeStruct
    vmem = pltpu.VMEM
    return per_canvas_call(
        functools.partial(mlp_kernel, grid_rows, grid_cols),
        "feed_forward",
        group,
        [
            sec, Held(top), Held(bot), Whole(hm), Whole(vm), Whole(aug), Whole(aug_rows), Whole(cot), att,
        ],
        [fc1, dwv, fc2h, vecs],
        [
            Whole(sds(cot.shape, bf16)),
            sds((canvases, tokens, C), f32),
            sds((canvases, grid_cols, C), bf16),
            sds((canvases, grid_cols, C), bf16),
        ],
        [
            sds((C, FF), f32),
            sds((16, FF), f32),
            sds((C, FF), f32),
            sds((8, C), f32),
        ],
        [
            vmem((4, K3 + C, FF), bf16),
            vmem((4, FF, K3), bf16),
            vmem((C, FF), bf16),
            vmem((4, stacked // 2, K3 + C), bf16),
            vmem((4, K3, stacked // 2), bf16),
            vmem((4, K3, FF), f32),
            vmem((32, FF), f32),
            vmem((stacked, FF), bf16),
            vmem((4, stacked // 2, FF), bf16),
            vmem((4, stacked // 2, K3), f32),
        ],
        flops=9e9,
        earlier=[(0, x) for x in earlier],
        inside=True,
    )


def embed_back_kernel(
    grid_rows, grid_cols, parts, starts, ends,
    *refs,
):
    gpool = refs[:parts]
    (
        red, emb, gatt, gq, blk, patches, hm, vm, vecs, embed_w, q_w, sr_w,
        slots, gvec_att, gqw, gkv, gproj, gfc1, gdw, gfc2t, gfc2b,
    ) = refs[parts : parts + 21]
    gin_out, grim_out, own_out, *other_out = refs[parts + 21 : -6]
    un, pg, gsr_out, gemb_out, gvec_out, flat = refs[-6:]
    step = pl.program_id(0)
    pool_rows, pool_cols = grid_rows // 4, grid_cols // 4
    tokens = grid_rows * grid_cols
    vec = lambda name: vecs[VEC[name] : VEC[name] + 1, :]

    @when_first(starts)
    def _():
        gsr_out[...] = jnp.zeros_like(gsr_out)
        gemb_out[...] = jnp.zeros_like(gemb_out)
        gvec_out[...] = jnp.zeros_like(gvec_out)

    grad_pool = gpool[0][0, 0].astype(f32) + gpool[1][0, 0].astype(f32)
    for part in gpool[2:]:
        grad_pool = grad_pool + part[0].astype(f32)
    xhat, rstd = normalise(red[0])
    gvec_out[0] += fold_rows(grad_pool * xhat)
    gvec_out[1] += fold_rows(grad_pool)
    grad_red = normalise_back(grad_pool, vec("srn_g"), xhat, rstd).astype(bf16)
    gvec_out[2] += fold_rows(grad_red.astype(f32))
    gsr_out[...] += mm_tn(blk[0], grad_red)
    block_grad = mm_nt(grad_red, sr_w[...])
    for r in range(pool_rows):
        for di in range(4):
            for dj in range(4):
                k = 4 * di + dj
                start = (4 * r + di) * grid_cols + dj
                un[pl.ds(start, pool_cols, stride=4), :] = block_grad[
                    r * pool_cols : (r + 1) * pool_cols, k * C : (k + 1) * C
                ]
    grad_normed = mm_nt(gq[0], q_w[...]) + un[0:tokens, :]
    xhat0, rstd0 = normalise(emb[0])
    base = xhat0 * vec("embed_g") + vec("embed_beta")
    xhat1, rstd1 = normalise(base)
    gvec_out[3] += fold_rows(grad_normed * xhat1)
    gvec_out[4] += fold_rows(grad_normed)
    grad_base = gatt[0] + normalise_back(grad_normed, vec("norm1_g"), xhat1, rstd1)
    gvec_out[5] += fold_rows(grad_base * xhat0)
    gvec_out[6] += fold_rows(grad_base)
    grad_emb = normalise_back(grad_base, vec("embed_g"), xhat0, rstd0).astype(bf16)
    grad_emb_f = grad_emb.astype(f32)
    gvec_out[7] += fold_rows(grad_emb_f)
    gemb_out[...] += mm(grad_emb_f.T.astype(bf16), patches[0])
    pg[...] = mm_nt(grad_emb, embed_w[...])
    left = hm[0, 0]

    def row(r):
        return slice(r * grid_cols, (r + 1) * grid_cols)

    for a in (1, 2):
        side = pg[:, (3 + a) * C : (4 + a) * C] * left[grid_cols : grid_cols + tokens].astype(f32)
        total = pg[:, a * C : (a + 1) * C] + pltpu.roll(side, tokens - 1, 0)
        for r in range(grid_rows):
            gin_out[0, r, a - 1] = total[row(r)]
    rows = []
    sides = []
    for r in range(grid_rows):
        middle = pg[row(r), 0:C]
        side = pg[row(r), 3 * C : 4 * C] * left[row(r)].astype(f32)
        if r % 4 == 0:
            keep = vm[0, 2 * (r // 4)].astype(f32)
            middle = middle * keep
            side = side * keep
        rows.append(middle)
        sides.append(side)
    above = jnp.concatenate(rows, axis=0) + pltpu.roll(
        jnp.concatenate(sides, axis=0), tokens - 1, 0
    )
    grim_out[0] = above[row(0)].astype(bf16)
    for r in range(1, grid_rows):
        gin_out[0, r - 1, 1] += above[row(r)]

    @pl.when(step == pl.num_programs(0) - 1)
    def _():
        if ends:
            pack_into(
                slots, gemb_out, gvec_out, gvec_att, gqw, gkv, gsr_out, gproj, gfc1, gdw, gfc2t,
                gfc2b, own_out, other_out[0] if other_out else None, flat,
            )


def embed_back_call(
    group, feat, gpool, red, emb, gatt, gq, blk, patches, hm, vm, vecs, embed_w, q_w, sr_w,
    slots, grads, total, half,
):
    canvases = group.count
    _, grid_rows, _, grid_cols, _ = feat.shape
    tokens = grid_rows * grid_cols
    sds = jax.ShapeDtypeStruct
    return per_canvas_call(
        functools.partial(embed_back_kernel, grid_rows, grid_cols, len(gpool)),
        "embed_back",
        group,
        [Held(x, k < 2) for k, x in enumerate(gpool)] + [red, emb, gatt, gq, blk, patches, Whole(hm), Whole(vm)],
        [vecs, embed_w, q_w, sr_w, slots] + list(grads),
        [
            Whole(sds(feat.shape, f32)),
            Whole(sds((feat.shape[0], grid_cols, C), bf16)),
        ],
        [sds(half, f32), sds(half, bf16)] if half[0] > 1 else [sds(half, f32)],
        [
            pltpu.VMEM((tokens + SPARE, C), f32),
            pltpu.VMEM((tokens, KEMB), f32),
            pltpu.VMEM((16 * C, C), f32),
            pltpu.VMEM((C, KEMB), f32),
            pltpu.VMEM((8, 8, C), f32),
            pltpu.VMEM((total + SPARE, C), f32),
        ],
        flops=3e9,
    )


def add_rim_kernel(grad_in, rim_in, grad_out):
    grad_out[:, 0, 0] = grad_in[:, 0, 0] + rim_in[...].astype(f32)


def add_rim_call(grad, rim):
    canvases, grid_rows, _, grid_cols, pair_ch = grad.shape
    block = pl.BlockSpec(
        (canvases, 1, 1, grid_cols, pair_ch), lambda i: (0, grid_rows - 1, 1, 0, 0)
    )
    return pl.pallas_call(
        add_rim_kernel,
        grid=(1,),
        in_specs=[block, whole_block(rim.shape)],
        out_specs=block,
        out_shape=jax.ShapeDtypeStruct(grad.shape, f32),
        input_output_aliases={0: 0},
        name="add_rim",
    )(grad, rim)


def flat_rows():
    starts, at = {}, 0
    for name, shape in param_layout():
        starts[name] = at
        at += math.prod(shape) // C
    return starts, at


def unpack_kernel(
    slots, near, far, vecs, embed_w, q_w, kv_w, sr_w, proj_w, fc1, dwv, fc2h, flat
):
    half = near.shape[0]
    if half == 1:
        flat[0 : near.shape[1], :] = near[0].astype(f32)
    else:
        rows = (flat.shape[0] - SPARE) // (2 * half)
        first = slots[half] == 0
        for s in range(half):
            here, there = near[slots[s]][:rows], far[slots[s]][:rows]
            even, odd = 2 * s * rows, (2 * s + 1) * rows
            flat[even : even + rows, :] = jnp.where(first, here, there).astype(f32)
            flat[odd : odd + rows, :] = jnp.where(first, there, here).astype(f32)
    at, _ = flat_rows()

    def take(name, start, count):
        return flat[at[name] + start : at[name] + start + count, :]

    for i, name in enumerate(VEC_NAMES):
        vecs[i : i + 1, :] = take(name, 0, 1)
    vecs[len(VEC_NAMES) :, :] = jnp.zeros((16 - len(VEC_NAMES), C), f32)
    for a in range(3):
        embed_w[a * C : (a + 1) * C, :] = take("embed_w", a * 3 * C_IN + C_IN, C).astype(bf16)
        left = take("embed_w", a * 3 * C_IN, C_IN)
        embed_w[(3 + a) * C : (4 + a) * C, :] = jnp.concatenate(
            [jnp.zeros_like(left), left], axis=0
        ).astype(bf16)
    q_w[...] = take("q_w", 0, C).astype(bf16)
    kv_w[:, :C] = take("k_w", 0, C).astype(bf16)
    kv_w[:, C:] = take("v_w", 0, C).astype(bf16)
    sr_w[...] = take("sr_w", 0, 16 * C).astype(bf16)
    proj_w[...] = take("proj_w", 0, C).astype(bf16)
    fc2h[...] = (take("fc2_w", 0, FF) * 0.5).astype(bf16)
    dwv[...] = jnp.zeros_like(dwv)
    for c in range(FF // C):
        lanes = slice(c * C, (c + 1) * C)
        fc1[:, lanes] = flat[pl.ds(at["fc1_w"] + c, C, stride=FF // C), :].astype(bf16)
        for k in range(9):
            dwv[k : k + 1, lanes] = take("dw_w", k * (FF // C) + c, 1)
            dwv[16 + k : 17 + k, lanes] = take("fc1_b", c, 1)
        dwv[9:10, lanes] = take("dw_b", c, 1)
    dwv[25:26, :] = jnp.ones((1, FF), f32)


def unpack_call(slots, total, near, far):
    vmem_block = pl.BlockSpec(memory_space=pltpu.VMEM)
    sds = jax.ShapeDtypeStruct
    shapes = [
        sds((16, C), f32),
        sds((KEMB, C), bf16),
        sds((C, C), bf16),
        sds((C, 2 * C), bf16),
        sds((16 * C, C), bf16),
        sds((C, C), bf16),
        sds((C, FF), bf16),
        sds((32, FF), f32),
        sds((FF, C), bf16),
    ]
    return pl.pallas_call(
        unpack_kernel,
        in_specs=[pl.BlockSpec(memory_space=pltpu.SMEM), vmem_block, vmem_block],
        out_specs=[vmem_block] * len(shapes),
        out_shape=shapes,
        scratch_shapes=[pltpu.VMEM((total + SPARE, C), f32)],
        compiler_params=pltpu.CompilerParams(vmem_limit_bytes=VMEM_LIMIT),
        name="unpack",
    )(
        slots,
        pltpu.with_memory_space_constraint(near, pltpu.VMEM),
        pltpu.with_memory_space_constraint(far, pltpu.VMEM),
    )


def pack_into(
    slots, gemb, gvec_emb, gvec_att, gqw, gkv, gsr, gproj, gfc1, gdw, gfc2t, gfc2b,
    own, other, flat,
):
    at, used = flat_rows()

    def put(name, start, value):
        flat[at[name] + start : at[name] + start + value.shape[0], :] = value

    def vec_row(ref, k):
        return jnp.sum(ref[k], axis=0, keepdims=True)

    emb = gemb[...].T
    for a in range(3):
        put("embed_w", a * 3 * C_IN + C_IN, emb[a * C : (a + 1) * C])
        put("embed_w", a * 3 * C_IN, emb[(3 + a) * C + C_IN : (4 + a) * C])
    for k, name in enumerate(
        ("srn_g", "srn_b", "sr_b", "norm1_g", "norm1_b", "embed_g", "embed_beta", "embed_b")
    ):
        put(name, 0, vec_row(gvec_emb, k))
    for k, name in enumerate(("norm2_g", "norm2_b", "proj_b", "q_b", "v_b")):
        put(name, 0, vec_row(gvec_att, k))
    put("q_w", 0, gqw[...])
    put("k_w", 0, gkv[:, :C])
    put("v_w", 0, gkv[:, C:])
    put("sr_w", 0, gsr[...])
    put("proj_w", 0, gproj[...])
    put("fc2_b", 0, jnp.sum(gfc2b[...], axis=0, keepdims=True))
    put("fc2_w", 0, gfc2t[...].T)
    for c in range(FF // C):
        lanes = slice(c * C, (c + 1) * C)
        flat[pl.ds(at["fc1_w"] + c, C, stride=FF // C), :] = gfc1[:, lanes]
        for k in range(9):
            put("dw_w", k * (FF // C) + c, gdw[k : k + 1, lanes])
        put("dw_b", c, gdw[9:10, lanes])
        put("fc1_b", c, gdw[10:11, lanes])
    total = flat.shape[0] - SPARE
    flat[used:total, :] = jnp.zeros((total - used, C), f32)
    if other is None:
        own[0] = flat[0:total, :]
        return
    rows = total // (2 * own.shape[0])
    blank = jnp.zeros((own.shape[1] - rows, C), f32)
    first = slots[own.shape[0]] == 0
    for s in range(own.shape[0]):
        even = flat[2 * s * rows : (2 * s + 1) * rows, :]
        odd = flat[(2 * s + 1) * rows : (2 * s + 2) * rows, :]
        here, there = jnp.where(first, even, odd), jnp.where(first, odd, even)
        own[slots[s]] = jnp.concatenate([here, blank], axis=0)
        other[slots[s]] = jnp.concatenate([there, blank], axis=0).astype(bf16)


def other_core(block):
    size = lax.axis_size("rows")
    return lax.ppermute(block, "rows", [(i, i ^ 1) for i in range(size)])


def along_z(block, distance):
    size = lax.axis_size("rows")
    chain = size // 2
    route = [(i, 2 * ((i // 2 + distance) % chain) + i % 2) for i in range(size)]
    return lax.ppermute(block, "rows", route)


def batch_partner(index, k, size):
    return index ^ k if size & (size - 1) == 0 else (index + k) % size


def along_batch(block, k):
    size = lax.axis_size("batch")
    return lax.ppermute(block, "batch", [(i, batch_partner(i, k, size)) for i in range(size)])


def batch_source(k, size):
    return k if size & (size - 1) == 0 else (size - k) % size


def gather_chain(block):
    return jnp.stack([block] + [along_z(block, k) for k in range(1, lax.axis_size("rows") // 2)])


def z_partner(block, k):
    size = lax.axis_size("rows")
    return lax.ppermute(block, "rows", [(i, 2 * ((i // 2) ^ k) + i % 2) for i in range(size)])


def sum_over_devices(value):
    chain, batches = lax.axis_size("rows") // 2, lax.axis_size("batch")
    if chain & (chain - 1) or batches & (batches - 1):
        return lax.psum(value, ("batch", "rows"))
    value = value + other_core(value)
    for size, move in ((chain, z_partner), (batches, along_batch)):
        parts = [value] + [move(value, k) for k in range(1, size)]
        while len(parts) > 1:
            parts = [parts[i] + parts[i + 1] for i in range(0, len(parts), 2)]
        value = parts[0]
    return value


def per_step(count, wanted):
    return max(n for n in range(1, wanted + 1) if count % n == 0)


def shift_rows(block, distance):
    size = lax.axis_size("rows")
    route = [(i, i + distance) for i in range(size) if 0 <= i + distance < size]
    return lax.ppermute(block, "rows", route)


def shards(
    features,
    cotangent,
    crop_ids,
    pooled_ids,
    master_weights,
    first_moment,
    second_moment,
    weight_average,
):
    canvases, double_rows, grid_cols, pair_ch = features.shape
    grid_rows = double_rows // 2
    pool_rows, pool_cols = grid_rows // 4, grid_cols // 4
    tokens = grid_rows * grid_cols

    chain, batches = lax.axis_size("rows") // 2, lax.axis_size("batch")
    pieces = 2 * chain * batches
    part_len = master_weights.shape[0]
    total_params = part_len * pieces
    low = master_weights.astype(bf16)
    aligned = part_len % C == 0
    padded_rows = (part_len // C + 7) // 8 * 8
    if aligned:
        low = low.reshape(part_len // C, C)
        low = jnp.pad(low, ((0, padded_rows - part_len // C), (0, 0)))
    low = gather_chain(low)
    low = jnp.stack([low] + [along_batch(low, k) for k in range(1, batches)])
    row_index, batch_index = lax.axis_index("rows"), lax.axis_index("batch")
    core, z_index = row_index % 2, row_index // 2
    piece = jnp.arange(pieces, dtype=jnp.int32)
    piece_core, piece_z = piece % 2, piece // 2 % chain
    piece_batch = piece // (2 * chain)
    if batches & (batches - 1) == 0:
        batch_slot = piece_batch ^ batch_index
    else:
        batch_slot = (batch_index - piece_batch) % batches
    half_slot = batch_slot * chain + (z_index - piece_z) % chain
    slots = (piece_core ^ core) * (batches * chain) + half_slot
    pair_slots = jnp.concatenate([half_slot[::2], core[None]])
    feat = features.reshape(canvases, grid_rows, 2, grid_cols, pair_ch)
    rim = shift_rows(features[:, double_rows - 1], 1)
    above_ids = shift_rows(pooled_ids[:, pool_rows - 1], 1)
    above_ids = jnp.where(row_index == 0, -1, above_ids)
    below_ids = shift_rows(pooled_ids[:, 0], -1)
    below_ids = jnp.where(row_index == 2 * chain - 1, -1, below_ids)
    idr = jnp.concatenate(
        [
            jnp.repeat(above_ids, 4, axis=1),
            crop_ids.reshape(canvases, tokens),
            jnp.repeat(below_ids, 4, axis=1),
        ],
        axis=1,
    )
    extended = tokens + 2 * grid_cols
    idr = jnp.pad(idr, ((0, 0), (0, lane_pad(extended) - extended)), constant_values=-1)
    idr = idr[:, None]
    own_ids = pooled_ids.reshape(canvases, pool_rows * pool_cols)
    own_ids = jnp.pad(own_ids, ((0, 0), (0, C - pool_rows * pool_cols)))[:, None]

    every = Group(canvases, 0)
    hm, vm = near_masks_call(every, grid_rows, grid_cols, idr)
    low, hm, vm, own_ids, rim, pair_slots = lax.optimization_barrier(
        (low, hm, vm, own_ids, rim, pair_slots)
    )
    far_low = other_core(low)
    if aligned:
        low = low.reshape(pieces // 2, padded_rows, C)
        far_low = far_low.reshape(low.shape)
    else:
        both = jnp.stack([low, far_low]).reshape(pieces, part_len)
        low = jnp.take(both, slots, axis=0).reshape(1, total_params // C, C)
        far_low = low[:, :8]
    vecs, embed_w, q_w, kv_w, sr_w, proj_w, fc1, dwv, fc2h = unpack_call(
        pair_slots, total_params // C, low, far_low
    )

    cot = cotangent.reshape(canvases, tokens, C)
    groups = [every]
    embed_group = Group(canvases, 0, per_step(canvases, EMBED_PER))
    attend_group = Group(canvases, 0, per_step(canvases, ATTEND_PER))
    attend_back_group = Group(canvases, 0, per_step(canvases, ATTEND_BACK_PER))
    embed_back_group = Group(canvases, 0, per_step(canvases, EMBED_BACK_PER))
    embedded, chains, gathered = [], [], []
    for group in groups:
        embedded.append(embed_call(embed_group, feat, rim, hm, vm, own_ids, vecs, embed_w, q_w, sr_w))
        chains.append(gather_chain(embedded[-1][6]))
    late_idr, _ = lax.optimization_barrier((idr, embedded[-1][6]))
    token_masks = token_masks_call(every, grid_rows, grid_cols, late_idr)
    chains[-1], token_masks = lax.optimization_barrier((chains[-1], token_masks))
    q_hot, aug, aug_rows = token_masks
    gathered = [(near, other_core(near)) for near in chains]
    attended, halos = [], []
    for group, (_, base, _, q, _, _, _, _), (near, far) in zip(groups, embedded, gathered):
        attended.append(attend_call(attend_group, grid_cols, q, near, far, q_hot, base, vecs, kv_w, proj_w))
        _, _, _, _, _, head, tail = attended[-1]
        halos.append((shift_rows(tail, 1), shift_rows(head, -1)))
    layer_out, fed, back_halos = (), [], []
    for group, (_, _, _, att, sec, _, _), (top, bot) in zip(groups, attended, halos):
        wide = Group(group.count, group.first, per_step(canvases, MLP_PER))
        out = mlp_call(
            wide, sec, top, bot, hm, vm, aug, aug_rows, cot, att, fc1, dwv, fc2h, vecs, layer_out
        )
        layer_out = (out[0],)
        fed.append(out)
        back_halos.append((shift_rows(out[3], 1), shift_rows(out[2], -1)))
    backs, pool_parts = [], []
    for g, group in enumerate(groups):
        emb, _, normed, q, blk, red, _, patches = embedded[g]
        exp_scores, mix, inv, att = attended[g][:4]
        out = attend_back_call(
            attend_back_group, fed[g][1], *back_halos[g], att, cot, mix, inv, exp_scores, q, normed,
            *gathered[g], vecs, kv_w, proj_w,
        )
        backs.append(out)
        mine, theirs = out[2], other_core(out[3])
        pool_parts.append([mine, theirs])
        for k in range(1, chain):
            both = mine[k].astype(f32) + theirs[k].astype(f32)
            pool_parts[-1].append(along_z(both.astype(bf16), -k))
    emb, _, _, _, blk, red, _, patches = embedded[0]
    gatt, gq, _, _, g_proj_w, g_kv_w, g_q_w, gvec_att = backs[0]
    half = (pieces // 2, padded_rows, C) if aligned else (1, total_params // C, C)
    g_in, grim, own, *other = embed_back_call(
        embed_back_group, feat, pool_parts[0], red, emb, gatt, gq, blk, patches, hm, vm,
        vecs, embed_w, q_w, sr_w,
        pair_slots, [gvec_att, g_q_w, g_kv_w, g_proj_w, *fed[0][4:]], total_params // C, half,
    )
    layer_out = layer_out[0]
    input_grad = add_rim_call(g_in, shift_rows(grim, -1))

    if aligned:
        own = own.reshape(batches, chain, padded_rows, C)
        other = other[0].reshape(batches, chain, padded_rows, C)
    else:
        order = jnp.zeros((pieces,), jnp.int32).at[slots].set(piece)
        both = jnp.take(own.reshape(pieces, part_len), order, axis=0)
        both = both.reshape(2, batches, chain, part_len)
        own, other = both[0], both[1].astype(bf16)
    own = own + other_core(other).astype(f32)
    own = sum(
        [
            along_batch(own[batch_source(k, batches)].astype(bf16), k).astype(f32)
            for k in range(1, batches)
        ],
        own[0],
    )
    own, input_grad = lax.optimization_barrier((own, input_grad))
    input_grad = input_grad.reshape(features.shape)
    shard_grad = sum(
        [along_z(own[k].astype(bf16), -k).astype(f32) for k in range(1, chain)], own[0]
    )
    if aligned:
        squares = jnp.sum((shard_grad * shard_grad).reshape(-1, 8, C), axis=0)
    else:
        squares = jnp.broadcast_to(jnp.sum(shard_grad * shard_grad) / (8 * C), (8, C))
    square_sum = jnp.sum(sum_over_devices(squares))
    if aligned:
        shard_grad = shard_grad[: part_len // C]
    shard_grad = shard_grad.reshape(part_len)
    grad_norm = jnp.sqrt(square_sum)
    clip_limit = math.sqrt(total_params)
    clipped = shard_grad * (clip_limit / jnp.maximum(grad_norm, clip_limit))
    new_first = BETA_ONE * first_moment + (1.0 - BETA_ONE) * clipped
    new_second = BETA_TWO * second_moment + (1.0 - BETA_TWO) * clipped * clipped
    first_hat = new_first / (1.0 - BETA_ONE**UPDATES)
    second_hat = new_second / (1.0 - BETA_TWO**UPDATES)
    new_weights = master_weights * (1.0 - LEARN_RATE * DECAY_RATE) - LEARN_RATE * first_hat / (
        jnp.sqrt(second_hat) + ADAM_EPS
    )
    new_average = AVERAGE_KEEP * weight_average + (1.0 - AVERAGE_KEEP) * new_weights
    layer_out = layer_out.reshape(cotangent.shape)
    return (layer_out, input_grad, grad_norm, new_first, new_second, new_weights, new_average)


def solution(mesh):
    placed = (
        P("batch", "rows", None, None),
        P("batch", "rows", None, None),
        P("batch", "rows", None),
        P("batch", "rows", None),
        P(("batch", "rows")),
        P(("batch", "rows")),
        P(("batch", "rows")),
        P(("batch", "rows")),
    )
    return jax.shard_map(
        shards,
        mesh=mesh,
        in_specs=placed,
        out_specs=(
            P("batch", "rows", None, None),
            P("batch", "rows", None, None),
            P(),
            P(("batch", "rows")),
            P(("batch", "rows")),
            P(("batch", "rows")),
            P(("batch", "rows")),
        ),
        check_vma=False,
    )
```

```python
import functools
import math

import jax
import jax.numpy as jnp
from jax import lax
from jax.experimental import pallas as pl
from jax.experimental.pallas import tpu as pltpu
from jax.sharding import PartitionSpec as P

C_IN = 64
C = 128
HEADS = 2
FF = 1024
HEAD_DIM = 64
UPDATES = 10

NORM_EPS = 1e-06
BETA_ONE = 0.9
BETA_TWO = 0.999
LEARN_RATE = 0.1
DECAY_RATE = 0.05
ADAM_EPS = 1e-08
AVERAGE_KEEP = 0.9
MASKED = -1e30
ROOT_HALF = 0.7071067811865476
LOG2E = 1.4426950408889634
PDF_SHIFT = math.log2(2.0 / math.sqrt(math.pi))
KEMB = 6 * C
K3 = 3 * C

f32 = jnp.float32
bf16 = jnp.bfloat16
VMEM_LIMIT = 60 * 2**20
SPARE = 32
MLP_PER = 1
EMBED_PER = 1
ATTEND_PER = 1
ATTEND_BACK_PER = 1
EMBED_BACK_PER = 1

VEC_NAMES = (
    "embed_b", "embed_g", "embed_beta", "norm1_g", "norm1_b", "q_b", "v_b", "sr_b",
    "srn_g", "srn_b", "proj_b", "norm2_g", "norm2_b", "fc2_b",
)
VEC = {name: i for i, name in enumerate(VEC_NAMES)}


def param_layout():
    return [
        ("embed_w", (9 * C_IN, C)),
        ("embed_b", (C,)),
        ("embed_g", (C,)),
        ("embed_beta", (C,)),
        ("norm1_g", (C,)),
        ("norm1_b", (C,)),
        ("q_w", (C, C)),
        ("q_b", (C,)),
        ("k_w", (C, C)),
        ("v_w", (C, C)),
        ("v_b", (C,)),
        ("sr_w", (16 * C, C)),
        ("sr_b", (C,)),
        ("srn_g", (C,)),
        ("srn_b", (C,)),
        ("proj_w", (C, C)),
        ("proj_b", (C,)),
        ("norm2_g", (C,)),
        ("norm2_b", (C,)),
        ("fc1_w", (C, FF)),
        ("fc1_b", (FF,)),
        ("dw_w", (9, FF)),
        ("dw_b", (FF,)),
        ("fc2_w", (FF, C)),
        ("fc2_b", (C,)),
    ]


def mm(left, right):
    return jnp.dot(left, right, preferred_element_type=f32)


def mm_nt(left, right):
    return lax.dot_general(
        left, right, (((1,), (1,)), ((), ())), preferred_element_type=f32
    )


def mm_tn(left, right):
    return lax.dot_general(
        left, right, (((0,), (0,)), ((), ())), preferred_element_type=f32
    )


def split_hi_lo(value):
    high = value.astype(bf16)
    return high, (value - high.astype(f32)).astype(bf16)


def normalise(value):
    centre = value - jnp.mean(value, axis=-1, keepdims=True)
    rstd = lax.rsqrt(jnp.mean(centre * centre, axis=-1, keepdims=True) + NORM_EPS)
    return centre * rstd, rstd


def normalise_back(grad, gain, xhat, rstd):
    scaled = grad * gain
    first = jnp.mean(scaled, axis=-1, keepdims=True)
    other = jnp.mean(scaled * xhat, axis=-1, keepdims=True)
    return rstd * (scaled - first - xhat * other)


def fold_rows(value):
    return jnp.sum(value.reshape(value.shape[0] // 8, 8, value.shape[1]), axis=0)


def lane_pad(count):
    return (count + C - 1) // C * C


def crop_columns(idr, grid_cols):
    ids = jnp.broadcast_to(idr[0], (8, idr.shape[2]))
    width = ids.shape[1]
    column = lax.broadcasted_iota(jnp.int32, ids.shape, 1) % grid_cols
    kind = lax.broadcasted_iota(jnp.int32, ids.shape, 0)
    left = (ids == pltpu.roll(ids, 1, 1)) & (column != 0)
    right = (ids == pltpu.roll(ids, width - 1, 1)) & (column != grid_cols - 1)
    upper = ids == pltpu.roll(ids, grid_cols, 1)
    lower = ids == pltpu.roll(ids, width - grid_cols, 1)
    rows = jnp.zeros(ids.shape, f32)
    for k, same in enumerate((left, right, upper, lower)):
        rows = jnp.where((kind == k) & same, 1.0, rows)
    return rows.T


def spread(columns, k, start, count):
    return jnp.broadcast_to(columns[start : start + count, k : k + 1], (count, C))


def tap_rows(idr, grid_cols):
    ids = jnp.broadcast_to(idr[0], (32, idr.shape[2]))
    width = ids.shape[1]
    column = lax.broadcasted_iota(jnp.int32, ids.shape, 1) % grid_cols
    kind = lax.broadcasted_iota(jnp.int32, ids.shape, 0) % 16
    rows = jnp.where(kind == 9, 1.0, jnp.zeros(ids.shape, f32))
    for a in (-1, 0, 1):
        for b in (-1, 0, 1):
            k = 3 * (a + 1) + b + 1
            away = (-(a * grid_cols + b)) % width
            same = ids == (pltpu.roll(ids, away, 1) if away else ids)
            inside = (column + b >= 0) & (column + b < grid_cols)
            rows = jnp.where((kind == k) & same & inside, 1.0, rows)
    return pltpu.roll(rows, width - grid_cols, 1)


def one_hot_digits(low, high):
    lane = lax.broadcasted_iota(jnp.int32, (low.shape[0], C), 1).astype(f32)
    return (lane == low) | (lane == high + 32.0)


def when_first(starts):
    def run(body):
        if starts:
            pl.when(pl.program_id(0) == 0)(body)

    return run


class Stack:
    def __init__(self, value):
        self.value = value
        self.shape = value.shape


class Whole:
    def __init__(self, value):
        self.value = value
        self.shape = value.shape


class Held:
    def __init__(self, value, behind=False):
        self.value, self.behind = value, behind
        self.shape = value.shape


class Group:
    def __init__(self, count, first, per=1):
        self.count, self.first, self.per = count, first, per


def canvas_block(array, group):
    shape, per = array.shape, group.per
    at = group.first // per if isinstance(array, Whole) else 0
    if isinstance(array, Held):
        return pl.BlockSpec(memory_space=pltpu.VMEM)
    if isinstance(array, Stack):
        return pl.BlockSpec((shape[0], per) + shape[2:], lambda i: (0, i) + (0,) * (len(shape) - 2))
    return pl.BlockSpec((per,) + shape[1:], lambda i: (i + at,) + (0,) * (len(shape) - 1))


def bare(array):
    return array.value if isinstance(array, (Stack, Whole, Held)) else array


def whole_block(shape):
    return pl.BlockSpec(shape, lambda i: (0,) * len(shape))


def per_canvas_call(
    kernel, name, group, canvas_in, shared_in, canvas_out, shared_out, scratch, flops=0, earlier=(),
    inside=False,
):
    steps = group.count // group.per
    inputs = [
        pltpu.with_memory_space_constraint(x.value, pltpu.VMEM) if isinstance(x, Held) else bare(x)
        for x in canvas_in
    ] + list(shared_in)
    outputs = [bare(x) for x in canvas_out] + list(shared_out)
    in_specs = [canvas_block(x, group) for x in canvas_in]
    in_specs += [
        pl.BlockSpec(memory_space=pltpu.SMEM) if x.ndim == 1 else whole_block(x.shape)
        for x in shared_in
    ]
    aliases = {}
    if earlier:
        aliases = {len(inputs) + k: place for k, (place, _) in enumerate(earlier)}
        skip = slice(len(inputs), len(inputs) + len(earlier))
        in_specs += [pl.BlockSpec(memory_space=pl.ANY)] * len(earlier)
        inputs += [array for _, array in earlier]

    else:
        skip = slice(len(inputs), len(inputs))

    def body(*refs):
        refs = list(refs[: skip.start] + refs[skip.stop :])
        out_at = len(canvas_in) + len(shared_in)
        per_canvas = list(enumerate(canvas_in)) + [
            (out_at + k, x) for k, x in enumerate(canvas_out)
        ]
        if inside:
            views = list(refs)
            for k, x in per_canvas:
                if isinstance(x, Held):
                    views[k] = refs[k].at[pl.ds(pl.program_id(0) * group.per, group.per)]
            kernel(*views)
            return
        for p in range(group.per):
            views = list(refs)
            for k, x in per_canvas:
                behind = isinstance(x, Stack) or (isinstance(x, Held) and x.behind)
                at = pl.ds(pl.program_id(0) * group.per + p, 1) if isinstance(x, Held) else pl.ds(p, 1)
                views[k] = refs[k].at[:, at] if behind else refs[k].at[at]
            kernel(p == 0, p == group.per - 1, *views)

    bytes_moved = sum(x.size * x.dtype.itemsize for x in inputs) + sum(
        math.prod(x.shape) * x.dtype.itemsize for x in outputs
    )
    return pl.pallas_call(
        body,
        grid=(steps,),
        in_specs=in_specs,
        out_specs=[canvas_block(x, group) for x in canvas_out]
        + [whole_block(x.shape) for x in shared_out],
        out_shape=outputs,
        scratch_shapes=scratch,
        input_output_aliases=aliases,
        compiler_params=pltpu.CompilerParams(vmem_limit_bytes=VMEM_LIMIT),
        cost_estimate=pl.CostEstimate(
            flops=int(flops * group.count), bytes_accessed=int(bytes_moved), transcendentals=0
        ),
        name=name,
    )(*inputs)


def near_masks_kernel(grid_rows, grid_cols, starts, ends, idr, hm_out, vm_out):
    columns = crop_columns(idr, grid_cols)
    extended = (grid_rows + 2) * grid_cols
    for k in range(2):
        hm_out[0, k] = spread(columns, k, 0, extended).astype(bf16)
    for r in range(0, grid_rows, 4):
        k = 2 * (r // 4)
        vm_out[0, k] = spread(columns, 2, (r + 1) * grid_cols, grid_cols).astype(bf16)
        vm_out[0, k + 1] = spread(columns, 3, (r + 4) * grid_cols, grid_cols).astype(bf16)


def near_masks_call(group, grid_rows, grid_cols, idr):
    canvases = idr.shape[0]
    sds = jax.ShapeDtypeStruct
    return per_canvas_call(
        functools.partial(near_masks_kernel, grid_rows, grid_cols),
        "near_masks",
        group,
        [idr],
        [],
        [
            sds((canvases, 2, (grid_rows + 2) * grid_cols, C), bf16),
            sds((canvases, grid_rows // 2, grid_cols, C), bf16),
        ],
        [],
        [],
    )


def token_masks_kernel(grid_cols, starts, ends, idr, hot_out, aug_out, row_out):
    tokens = hot_out.shape[1]
    ids = jnp.broadcast_to(idr[0], (8, idr.shape[2]))
    kind = lax.broadcasted_iota(jnp.int32, ids.shape, 0)
    column = jnp.where(kind == 0, ids % 32, ids // 32).astype(f32).T
    column = column[grid_cols : grid_cols + tokens]
    hot = one_hot_digits(column[:, 0:1], column[:, 1:2])
    hot_out[0] = jnp.where(hot, 1.0, 0.0).astype(bf16)
    taps = tap_rows(idr, grid_cols)
    for q in range(2):
        rows = [taps[:, r * grid_cols : (r + 1) * grid_cols] for r in range(q, tokens // grid_cols, 2)]
        row_out[0, q] = jnp.concatenate(rows, axis=1).astype(bf16)
    aug_out[0, :, 0:32] = taps.T[:tokens].astype(bf16)
    aug_out[0, :, 32:] = jnp.zeros((tokens, C - 32), bf16)


def token_masks_call(group, grid_rows, grid_cols, idr):
    canvases, tokens = idr.shape[0], grid_rows * grid_cols
    sds = jax.ShapeDtypeStruct
    return per_canvas_call(
        functools.partial(token_masks_kernel, grid_cols),
        "token_masks",
        group,
        [idr],
        [],
        [
            sds((canvases, tokens, C), bf16),
            sds((canvases, tokens, C), bf16),
            sds((canvases, 2, 32, tokens // 2), bf16),
        ],
        [],
        [],
    )


def fill_patches(grid_rows, grid_cols, feat, rim, hm, vm, patches):
    tokens = grid_rows * grid_cols
    left = hm[0, 0]
    for a in range(3):
        rows = []
        for r in range(grid_rows):
            if a == 0:
                rows.append(rim[0] if r == 0 else feat[0, r - 1, 1])
            else:
                rows.append(feat[0, r, a - 1])
        source = jnp.concatenate(rows, axis=0)
        rolled = pltpu.roll(source.astype(f32), 1, 0)
        mask_at = 0 if a == 0 else grid_cols
        shifted = (rolled * left[mask_at : mask_at + tokens].astype(f32)).astype(bf16)
        if a == 0:
            for r in range(grid_rows):
                here = slice(r * grid_cols, (r + 1) * grid_cols)
                if r % 4 == 0:
                    keep = vm[0, 2 * (r // 4)]
                    patches[here, 0:C] = source[here] * keep
                    patches[here, 3 * C : 4 * C] = shifted[here] * keep
                else:
                    patches[here, 0:C] = source[here]
                    patches[here, 3 * C : 4 * C] = shifted[here]
        else:
            patches[:, a * C : (a + 1) * C] = source
            patches[:, (3 + a) * C : (4 + a) * C] = shifted


def embed_kernel(
    grid_rows, grid_cols, starts, ends,
    feat, rim, hm, vm, own_ids, vecs, embed_w, q_w, sr_w,
    emb_out, base_out, norm_out, q_out, blk_out, red_out, pool_out, patch_out,
    tok, blkf,
):
    pool_rows, pool_cols = grid_rows // 4, grid_cols // 4
    patches = patch_out.at[0]
    fill_patches(grid_rows, grid_cols, feat, rim, hm, vm, patches)
    vec = lambda name: vecs[VEC[name] : VEC[name] + 1, :]
    embedded = mm(patches[...], embed_w[...]) + vec("embed_b")
    emb_out[0] = embedded
    base = normalise(embedded)[0] * vec("embed_g") + vec("embed_beta")
    base_out[0] = base
    normed = (normalise(base)[0] * vec("norm1_g") + vec("norm1_b")).astype(bf16)
    norm_out[0] = normed
    queries = (mm(normed, q_w[...]) + vec("q_b")).astype(bf16)
    q_out[0] = queries * bf16(HEAD_DIM ** (-0.5))
    tok[0 : normed.shape[0], :] = normed.astype(f32)
    for r in range(pool_rows):
        for di in range(4):
            for dj in range(4):
                k = 4 * di + dj
                start = (4 * r + di) * grid_cols + dj
                blkf[r * pool_cols : (r + 1) * pool_cols, k * C : (k + 1) * C] = tok[
                    pl.ds(start, pool_cols, stride=4), :
                ]
    blocks = blkf[0 : pool_rows * pool_cols, :].astype(bf16)
    blk_out[0] = blocks
    reduced = mm(blocks, sr_w[...]) + vec("sr_b")
    red_out[0] = reduced
    own = pool_rows * pool_cols
    pooled = normalise(reduced)[0] * vec("srn_g") + vec("srn_b")
    ids = jnp.broadcast_to(own_ids[0], (8, C))
    kind = lax.broadcasted_iota(jnp.int32, ids.shape, 0)
    digits = jnp.where(kind == 0, ids % 32, jnp.where(kind == 1, ids // 32, 0)).astype(f32)
    pool_out[0] = jnp.concatenate([pooled, digits], axis=0).astype(bf16)


def embed_call(group, feat, rim, hm, vm, own_ids, vecs, embed_w, q_w, sr_w):
    canvases = group.count
    _, grid_rows, _, grid_cols, _ = feat.shape
    tokens = grid_rows * grid_cols
    own = tokens // 16
    sds = jax.ShapeDtypeStruct
    return per_canvas_call(
        functools.partial(embed_kernel, grid_rows, grid_cols),
        "embed",
        group,
        [Whole(feat), Held(rim), Whole(hm), Whole(vm), Whole(own_ids)],
        [vecs, embed_w, q_w, sr_w],
        [
            sds((canvases, tokens, C), f32),
            sds((canvases, tokens, C), f32),
            sds((canvases, tokens, C), bf16),
            sds((canvases, tokens, C), bf16),
            sds((canvases, own, 16 * C), bf16),
            sds((canvases, own, C), f32),
            sds((canvases, own + 8, C), bf16),
            sds((canvases, tokens, KEMB), bf16),
        ],
        [],
        [
            pltpu.VMEM((tokens + SPARE, C), f32),
            pltpu.VMEM((own + 8, 16 * C), f32),
        ],
        flops=2e9,
    )


def keys_values(pooled, kv_w, vecs):
    both = mm(pooled, kv_w)
    keys = both[:, :C].astype(bf16)
    values = (both[:, C:] + vecs[VEC["v_b"] : VEC["v_b"] + 1, :]).astype(bf16)
    return keys, values


def head_lanes(shape, head):
    lane = lax.broadcasted_iota(jnp.int32, shape, 1)
    return (lane // HEAD_DIM) == head


def all_pooled_rows(near, far):
    own = near.shape[2] - 8
    parts = [ref[k, 0].astype(f32) for ref in (near, far) for k in range(ref.shape[0])]
    return jnp.concatenate([part[:own] for part in parts], axis=0), [p[own:] for p in parts]


def attend_kernel(
    starts, ends,
    q, near, far, q_hot, base, vecs, kv_w, proj_w,
    exp_out, mix_out, inv_out, att_out, sec_out, head_out, tail_out,
):
    vec = lambda name: vecs[VEC[name] : VEC[name] + 1, :]
    pooled, digits = all_pooled_rows(near, far)
    keys, values = keys_values(pooled.astype(bf16), kv_w[...], vecs)
    values_t = values.astype(f32).T.astype(bf16)
    tokens = q.shape[1]
    own = near.shape[2] - 8
    columns = jnp.concatenate(digits, axis=0).T
    hot = [
        one_hot_digits(columns[:own, 8 * k : 8 * k + 1], columns[:own, 8 * k + 1 : 8 * k + 2])
        for k in range(len(digits))
    ]
    k_hot = jnp.where(jnp.concatenate(hot, axis=0), 0.0, MASKED).astype(bf16)
    q_cat = jnp.concatenate([q[0], q_hot[0]], axis=1)
    k_cat = []
    for h in range(HEADS):
        k_own = jnp.where(head_lanes(keys.shape, h), keys, jnp.zeros_like(keys))
        k_cat.append(jnp.concatenate([k_own, k_hot], axis=1))
    both_scores = mm_nt(jnp.concatenate(k_cat, axis=0), q_cat)
    total = keys.shape[0]
    for h in range(HEADS):
        scores = both_scores[h * total : (h + 1) * total]
        peak = jnp.max(scores, axis=0, keepdims=True)
        raised = jnp.exp(scores - peak)
        inverse = 1.0 / jnp.sum(raised, axis=0, keepdims=True)
        low = raised.astype(bf16)
        exp_out[0, h] = low
        inv_out[0, 4 * h : 4 * h + 4, :] = jnp.broadcast_to(inverse, (4, tokens))
        part = slice(h * HEAD_DIM, (h + 1) * HEAD_DIM)
        mix_out[0, part, :] = mm(values_t[part], low) * inverse
    mixed = mix_out[0].T.astype(bf16)
    attended = base[0] + mm(mixed, proj_w[...]) + vec("proj_b")
    att_out[0] = attended
    second = (normalise(attended)[0] * vec("norm2_g") + vec("norm2_b")).astype(bf16)
    sec_out[0] = second
    grid_cols = head_out.shape[1]
    head_out[0] = second[:grid_cols]
    tail_out[0] = second[tokens - grid_cols :]


def attend_call(group, grid_cols, q, near, far, q_hot, base, vecs, kv_w, proj_w):
    canvases, tokens, _ = q.shape
    total = 2 * near.shape[0] * (near.shape[2] - 8)
    sds = jax.ShapeDtypeStruct
    return per_canvas_call(
        attend_kernel,
        "attend",
        group,
        [q, Held(near, True), Held(far, True), Whole(q_hot), base],
        [vecs, kv_w, proj_w],
        [
            sds((canvases, HEADS, total, tokens), bf16),
            sds((canvases, C, tokens), f32),
            sds((canvases, 8, tokens), f32),
            sds((canvases, tokens, C), f32),
            sds((canvases, tokens, C), bf16),
            sds((canvases, grid_cols, C), bf16),
            sds((canvases, grid_cols, C), bf16),
        ],
        [],
        [],
        flops=2.5e9,
    )


def attend_back_kernel(
    grid_cols, starts, ends,
    gsec, gtop, gbot, att, cot, mix, inv, exp_in, q, normed, near, far, vecs, kv_w, proj_w,
    gatt_out, gq_out, gnear_out, gfar_out, gproj_out, gkv_out, gqw_out, gvec_out,
):
    step = pl.program_id(0)
    vec = lambda name: vecs[VEC[name] : VEC[name] + 1, :]

    @when_first(starts)
    def _():
        gproj_out[...] = jnp.zeros_like(gproj_out)
        gkv_out[...] = jnp.zeros_like(gkv_out)
        gqw_out[...] = jnp.zeros_like(gqw_out)
        gvec_out[...] = jnp.zeros_like(gvec_out)

    tokens = q.shape[1]
    last = tokens - grid_cols
    grad_second = jnp.concatenate(
        [
            gsec[0, :grid_cols] + gtop[0].astype(f32),
            gsec[0, grid_cols:last],
            gsec[0, last:] + gbot[0].astype(f32),
        ],
        axis=0,
    )
    xhat, rstd = normalise(att[0])
    gvec_out[0] += fold_rows(grad_second * xhat)
    gvec_out[1] += fold_rows(grad_second)
    grad_att = cot[0].astype(f32) + normalise_back(grad_second, vec("norm2_g"), xhat, rstd)
    gatt_out[0] = grad_att
    branch = grad_att.astype(bf16)
    gvec_out[2] += fold_rows(branch.astype(f32))
    mixed_t = mix[0]
    gproj_out[...] += mm(mixed_t.astype(bf16), branch)
    grad_mix_t = mm_nt(proj_w[...], branch)
    inverses = inv[0]
    pooled_f, _ = all_pooled_rows(near, far)
    keys, values = keys_values(pooled_f.astype(bf16), kv_w[...], vecs)
    keys_t = keys.astype(f32).T.astype(bf16)
    gq_parts = []
    gk_parts = []
    gv_parts = []
    for h in range(HEADS):
        part = slice(h * HEAD_DIM, (h + 1) * HEAD_DIM)
        scaled = (grad_mix_t[part] * inverses[4 * h : 4 * h + 1]).astype(bf16)
        middle = jnp.sum(scaled.astype(f32) * mixed_t[part], axis=0, keepdims=True)
        raised = exp_in[0, h]
        pair = jnp.concatenate([scaled, scaled], axis=0)
        gv_parts.append(mm_nt(raised, pair))
        v_own = jnp.where(head_lanes(values.shape, h), values, jnp.zeros_like(values))
        grad_p = mm(v_own, pair)
        grad_s = (raised.astype(f32) * (grad_p - middle)).astype(bf16)
        gq_parts.append(mm(keys_t[part], grad_s))
        gk_parts.append(mm(grad_s, q[0]))
    first = head_lanes(gk_parts[0].shape, 0)
    grad_keys = jnp.where(first, gk_parts[0], gk_parts[1])
    grad_values = jnp.where(first, gv_parts[0], gv_parts[1])
    grad_q = (jnp.concatenate(gq_parts, axis=0) * HEAD_DIM ** (-0.5)).T.astype(bf16)
    gq_out[0] = grad_q
    gvec_out[3] += fold_rows(grad_q.astype(f32))
    gvec_out[4] += fold_rows(grad_values)
    gqw_out[...] += mm_tn(normed[0], grad_q)
    k_high, k_low = split_hi_lo(grad_keys)
    v_high, v_low = split_hi_lo(grad_values)
    high = jnp.concatenate([k_high, v_high], axis=1)
    low = jnp.concatenate([k_low, v_low], axis=1)
    pooled_t = pooled_f.T.astype(bf16)
    gkv_out[...] += mm(pooled_t, high) + mm(pooled_t, low)
    grad_pool = mm_nt(high, kv_w[...]) + mm_nt(low, kv_w[...])
    chain, own = near.shape[0], near.shape[2] - 8
    for k in range(chain):
        gnear_out[k, 0] = grad_pool[k * own : (k + 1) * own].astype(bf16)
        gfar_out[k, 0] = grad_pool[(chain + k) * own : (chain + k + 1) * own].astype(bf16)


def attend_back_call(
    group, gsec, gtop, gbot, att, cot, mix, inv, exp_in, q, normed, near, far, vecs, kv_w, proj_w
):
    canvases, tokens, _ = q.shape
    sds = jax.ShapeDtypeStruct
    gpool = sds((near.shape[0], canvases, near.shape[2] - 8, C), bf16)
    return per_canvas_call(
        functools.partial(attend_back_kernel, gtop.shape[1]),
        "attend_back",
        group,
        [
            gsec, Held(gtop), Held(gbot), att, Whole(cot), mix, inv, exp_in, q, normed,
            Held(near, True), Held(far, True),
        ],
        [vecs, kv_w, proj_w],
        [
            sds((canvases, tokens, C), f32),
            sds((canvases, tokens, C), bf16),
            Stack(gpool),
            Stack(gpool),
        ],
        [
            sds((C, C), f32),
            sds((C, 2 * C), f32),
            sds((C, C), f32),
            sds((5, 8, C), f32),
        ],
        [],
        flops=3.5e9,
    )


def mlp_kernel(
    grid_rows, grid_cols,
    sec, top, bot, hm, vm, aug, aug_rows, cot, att, fc1, dwv, fc2h, vecs,
    lo, gsec, gtop, gbot, gfc1, gdw, gfc2t, gfc2b,
    wf, wt, f2t, xf, xt, acc, ones_grad, act, gm, gx,
):
    tokens = grid_rows * grid_cols
    half = tokens // 2
    pairs = grid_rows // 2
    extended = tokens + 2 * grid_cols
    step = pl.program_id(0)
    per = sec.shape[0]

    @pl.when(step == 0)
    def _():
        first = fc1[...].astype(f32)
        for b in range(3):
            rows = [first * (dwv[3 * a + b : 3 * a + b + 1, :] * ROOT_HALF) for a in range(3)]
            ends = (rows[0] + rows[2]) * 0.5
            mixed = [rows[0], ends + rows[1] * 0.5, ends - rows[1] * 0.5, rows[2]]
            for k in range(4):
                wf[k, b * C : (b + 1) * C, :] = mixed[k].astype(bf16)
        high, low = split_hi_lo(dwv[0:16, :] * dwv[16:32, :] * ROOT_HALF)
        for k in (0, 3):
            wf[k, K3 : K3 + 16, :] = high
            wf[k, K3 + 16 : K3 + 32, :] = low
            wf[k, K3 + 32 :, :] = jnp.zeros((C - 32, FF), bf16)
        for k in range(4):
            wt[k] = wf[k, :K3, :].T
        f2t[...] = fc2h[...].T
        acc[...] = jnp.zeros_like(acc)
        ones_grad[...] = jnp.zeros_like(ones_grad)
        gfc2t[...] = jnp.zeros_like(gfc2t)
        gfc2b[...] = jnp.zeros_like(gfc2b)

    def row(r):
        return slice(r * grid_cols, (r + 1) * grid_cols)

    def upper(r, p):
        return vm[p, 2 * (r // 4)].astype(f32) if r % 4 == 0 else None

    def lower(r, p):
        return vm[p, 2 * (r // 4) + 1].astype(f32) if r % 4 == 3 else None

    def kept(value, mask):
        return value if mask is None else value * mask

    for p in range(per):
        wide = jnp.concatenate(
            [top[p].astype(f32), sec[p].astype(f32), bot[p].astype(f32)], axis=0
        )
        for b in range(3):
            moved = wide
            if b != 1:
                moved = pltpu.roll(wide, 1 if b == 0 else extended - 1, 0)
                moved = moved * hm[p, b // 2].astype(f32)
            for i in range(pairs):
                d0, d1, d2, d3 = [moved[row(2 * i + k)] for k in range(4)]
                d0, d3 = kept(d0, upper(2 * i, p)), kept(d3, lower(2 * i + 1, p))
                at = slice(p * half + i * grid_cols, p * half + (i + 1) * grid_cols)
                for k, value in enumerate((d0 - d2, d1 + d2, d2 - d1, d1 - d3)):
                    xf[k, at, b * C : (b + 1) * C] = value.astype(bf16)
        mine = slice(p * half, (p + 1) * half)
        for k in range(4):
            xt[k, :, mine] = xf[k, mine, :K3].T
        for i in range(pairs):
            at = slice(p * half + i * grid_cols, p * half + (i + 1) * grid_cols)
            xf[0, at, K3:] = aug[p, row(2 * i)]
            xf[3, at, K3:] = -aug[p, row(2 * i + 1)]

    def by_parity(ref):
        return jnp.concatenate(
            [ref[p, row(2 * i + q)] for q in range(2) for p in range(per) for i in range(pairs)],
            axis=0,
        )

    given = by_parity(cot)
    m0 = mm(xf[0], wf[0])
    m1 = mm(xf[1, :, :K3], wf[1, :K3])
    m2 = mm(xf[2, :, :K3], wf[2, :K3])
    m3 = mm(xf[3], wf[3])
    d = mm(given, f2t[...])
    grads = []
    for q, u in enumerate((m0 + (m1 + m2), (m1 - m2) - m3)):
        at = slice(q * per * half, (q + 1) * per * half)
        phi = 1.0 + lax.erf(u)
        act[at, :] = (u * phi).astype(bf16)
        pdf = jnp.exp2(PDF_SHIFT - u * u * LOG2E)
        grads.append((phi + u * pdf) * d[at])
    even, odd = grads
    for k, value in enumerate((even, even + odd, even - odd, -odd)):
        gm[k] = value.astype(bf16)
    for k in range(4):
        acc[k] += mm(xt[k], gm[k])
        gx[k] = mm(gm[k], wt[k])
    for q in range(2):
        taps = jnp.concatenate([aug_rows[p, q] for p in range(per)], axis=1)
        ones_grad[...] += mm(taps, gm[3 * q] if q == 0 else -gm[3])
    given_f = given.astype(f32)
    gfc2t[...] += mm(given_f.T.astype(bf16), act[...])
    gfc2b[...] += fold_rows(given_f)
    mlp_out = mm(act[...], fc2h[...]) * (2 * ROOT_HALF) + vecs[VEC["fc2_b"] : VEC["fc2_b"] + 1, :]
    for p in range(per):
        total = None
        for b in range(3):
            rows = [None] * (grid_rows + 2)
            lanes = slice(b * C, (b + 1) * C)
            for i in range(pairs):
                at = slice(p * half + i * grid_cols, p * half + (i + 1) * grid_cols)
                c0, c1, c2, c3 = [gx[k, at, lanes] for k in range(4)]
                d0, d3 = kept(c0, upper(2 * i, p)), kept(-c3, lower(2 * i + 1, p))
                for k, value in enumerate((d0, (c1 - c2) + c3, (c1 + c2) - c0, d3)):
                    e = 2 * i + k
                    rows[e] = value if rows[e] is None else rows[e] + value
            side = jnp.concatenate(rows, axis=0)
            if b != 1:
                side = pltpu.roll(
                    side * hm[p, b // 2].astype(f32), extended - 1 if b == 0 else 1, 0
                )
            total = side if total is None else total + side
        total = total * (2 * ROOT_HALF)
        gtop[p] = total[0:grid_cols].astype(bf16)
        gsec[p] = total[grid_cols : grid_cols + tokens]
        gbot[p] = total[grid_cols + tokens :].astype(bf16)
        for i in range(pairs):
            for q in range(2):
                at = (q * per + p) * half + i * grid_cols
                r = row(2 * i + q)
                lo[p, r] = (att[p, r] + mlp_out[at : at + grid_cols]).astype(bf16)

    @pl.when(step == pl.num_programs(0) - 1)
    def _():
        first = fc1[...].astype(f32)
        summed = None
        bias = ones_grad[0:16, :]
        for b in range(3):
            lanes = slice(b * C, (b + 1) * C)
            both = (acc[1, lanes, :] + acc[2, lanes, :]) * 0.5
            apart = (acc[1, lanes, :] - acc[2, lanes, :]) * 0.5
            for a, tap in enumerate((acc[0, lanes, :] + both, apart, acc[3, lanes, :] + both)):
                k = 3 * a + b
                term = tap * dwv[k : k + 1, :]
                summed = term if summed is None else summed + term
                gdw[k : k + 1, :] = (
                    jnp.sum(tap * first, axis=0, keepdims=True) + bias[k : k + 1] * dwv[16:17, :]
                )
        gfc1[...] = summed
        gdw[9:10, :] = bias[9:10]
        gdw[10:11, :] = jnp.sum(bias[0:9] * dwv[0:9, :], axis=0, keepdims=True)
        gdw[11:16, :] = jnp.zeros((5, FF), f32)
        gfc2t[...] = gfc2t[...] * ROOT_HALF


def mlp_call(
    group, sec, top, bot, hm, vm, aug, aug_rows, cot, att, fc1, dwv, fc2h, vecs, earlier
):
    canvases, tokens, _ = sec.shape
    grid_cols = top.shape[1]
    grid_rows = tokens // grid_cols
    stacked = group.per * tokens
    sds = jax.ShapeDtypeStruct
    vmem = pltpu.VMEM
    return per_canvas_call(
        functools.partial(mlp_kernel, grid_rows, grid_cols),
        "feed_forward",
        group,
        [
            sec, Held(top), Held(bot), Whole(hm), Whole(vm), Whole(aug), Whole(aug_rows), Whole(cot), att,
        ],
        [fc1, dwv, fc2h, vecs],
        [
            Whole(sds(cot.shape, bf16)),
            sds((canvases, tokens, C), f32),
            sds((canvases, grid_cols, C), bf16),
            sds((canvases, grid_cols, C), bf16),
        ],
        [
            sds((C, FF), f32),
            sds((16, FF), f32),
            sds((C, FF), f32),
            sds((8, C), f32),
        ],
        [
            vmem((4, K3 + C, FF), bf16),
            vmem((4, FF, K3), bf16),
            vmem((C, FF), bf16),
            vmem((4, stacked // 2, K3 + C), bf16),
            vmem((4, K3, stacked // 2), bf16),
            vmem((4, K3, FF), f32),
            vmem((32, FF), f32),
            vmem((stacked, FF), bf16),
            vmem((4, stacked // 2, FF), bf16),
            vmem((4, stacked // 2, K3), f32),
        ],
        flops=9e9,
        earlier=[(0, x) for x in earlier],
        inside=True,
    )


def embed_back_kernel(
    grid_rows, grid_cols, parts, starts, ends,
    *refs,
):
    gpool = refs[:parts]
    (
        red, emb, gatt, gq, blk, patches, hm, vm, vecs, embed_w, q_w, sr_w,
        slots, gvec_att, gqw, gkv, gproj, gfc1, gdw, gfc2t, gfc2b,
    ) = refs[parts : parts + 21]
    gin_out, grim_out, own_out, *other_out = refs[parts + 21 : -6]
    un, pg, gsr_out, gemb_out, gvec_out, flat = refs[-6:]
    step = pl.program_id(0)
    pool_rows, pool_cols = grid_rows // 4, grid_cols // 4
    tokens = grid_rows * grid_cols
    vec = lambda name: vecs[VEC[name] : VEC[name] + 1, :]

    @when_first(starts)
    def _():
        gsr_out[...] = jnp.zeros_like(gsr_out)
        gemb_out[...] = jnp.zeros_like(gemb_out)
        gvec_out[...] = jnp.zeros_like(gvec_out)

    grad_pool = gpool[0][0, 0].astype(f32) + gpool[1][0, 0].astype(f32)
    for part in gpool[2:]:
        grad_pool = grad_pool + part[0].astype(f32)
    xhat, rstd = normalise(red[0])
    gvec_out[0] += fold_rows(grad_pool * xhat)
    gvec_out[1] += fold_rows(grad_pool)
    grad_red = normalise_back(grad_pool, vec("srn_g"), xhat, rstd).astype(bf16)
    gvec_out[2] += fold_rows(grad_red.astype(f32))
    gsr_out[...] += mm_tn(blk[0], grad_red)
    block_grad = mm_nt(grad_red, sr_w[...])
    for r in range(pool_rows):
        for di in range(4):
            for dj in range(4):
                k = 4 * di + dj
                start = (4 * r + di) * grid_cols + dj
                un[pl.ds(start, pool_cols, stride=4), :] = block_grad[
                    r * pool_cols : (r + 1) * pool_cols, k * C : (k + 1) * C
                ]
    grad_normed = mm_nt(gq[0], q_w[...]) + un[0:tokens, :]
    xhat0, rstd0 = normalise(emb[0])
    base = xhat0 * vec("embed_g") + vec("embed_beta")
    xhat1, rstd1 = normalise(base)
    gvec_out[3] += fold_rows(grad_normed * xhat1)
    gvec_out[4] += fold_rows(grad_normed)
    grad_base = gatt[0] + normalise_back(grad_normed, vec("norm1_g"), xhat1, rstd1)
    gvec_out[5] += fold_rows(grad_base * xhat0)
    gvec_out[6] += fold_rows(grad_base)
    grad_emb = normalise_back(grad_base, vec("embed_g"), xhat0, rstd0).astype(bf16)
    grad_emb_f = grad_emb.astype(f32)
    gvec_out[7] += fold_rows(grad_emb_f)
    gemb_out[...] += mm(grad_emb_f.T.astype(bf16), patches[0])
    pg[...] = mm_nt(grad_emb, embed_w[...])
    left = hm[0, 0]

    def row(r):
        return slice(r * grid_cols, (r + 1) * grid_cols)

    for a in (1, 2):
        side = pg[:, (3 + a) * C : (4 + a) * C] * left[grid_cols : grid_cols + tokens].astype(f32)
        total = pg[:, a * C : (a + 1) * C] + pltpu.roll(side, tokens - 1, 0)
        for r in range(grid_rows):
            gin_out[0, r, a - 1] = total[row(r)]
    rows = []
    sides = []
    for r in range(grid_rows):
        middle = pg[row(r), 0:C]
        side = pg[row(r), 3 * C : 4 * C] * left[row(r)].astype(f32)
        if r % 4 == 0:
            keep = vm[0, 2 * (r // 4)].astype(f32)
            middle = middle * keep
            side = side * keep
        rows.append(middle)
        sides.append(side)
    above = jnp.concatenate(rows, axis=0) + pltpu.roll(
        jnp.concatenate(sides, axis=0), tokens - 1, 0
    )
    grim_out[0] = above[row(0)].astype(bf16)
    for r in range(1, grid_rows):
        gin_out[0, r - 1, 1] += above[row(r)]

    @pl.when(step == pl.num_programs(0) - 1)
    def _():
        if ends:
            pack_into(
                slots, gemb_out, gvec_out, gvec_att, gqw, gkv, gsr_out, gproj, gfc1, gdw, gfc2t,
                gfc2b, own_out, other_out[0] if other_out else None, flat,
            )


def embed_back_call(
    group, feat, gpool, red, emb, gatt, gq, blk, patches, hm, vm, vecs, embed_w, q_w, sr_w,
    slots, grads, total, half,
):
    canvases = group.count
    _, grid_rows, _, grid_cols, _ = feat.shape
    tokens = grid_rows * grid_cols
    sds = jax.ShapeDtypeStruct
    return per_canvas_call(
        functools.partial(embed_back_kernel, grid_rows, grid_cols, len(gpool)),
        "embed_back",
        group,
        [Held(x, k < 2) for k, x in enumerate(gpool)] + [red, emb, gatt, gq, blk, patches, Whole(hm), Whole(vm)],
        [vecs, embed_w, q_w, sr_w, slots] + list(grads),
        [
            Whole(sds(feat.shape, f32)),
            Whole(sds((feat.shape[0], grid_cols, C), bf16)),
        ],
        [sds(half, f32), sds(half, bf16)] if half[0] > 1 else [sds(half, f32)],
        [
            pltpu.VMEM((tokens + SPARE, C), f32),
            pltpu.VMEM((tokens, KEMB), f32),
            pltpu.VMEM((16 * C, C), f32),
            pltpu.VMEM((C, KEMB), f32),
            pltpu.VMEM((8, 8, C), f32),
            pltpu.VMEM((total + SPARE, C), f32),
        ],
        flops=3e9,
    )


def add_rim_kernel(grad_in, rim_in, grad_out):
    grad_out[:, 0, 0] = grad_in[:, 0, 0] + rim_in[...].astype(f32)


def add_rim_call(grad, rim):
    canvases, grid_rows, _, grid_cols, pair_ch = grad.shape
    block = pl.BlockSpec(
        (canvases, 1, 1, grid_cols, pair_ch), lambda i: (0, grid_rows - 1, 1, 0, 0)
    )
    return pl.pallas_call(
        add_rim_kernel,
        grid=(1,),
        in_specs=[block, whole_block(rim.shape)],
        out_specs=block,
        out_shape=jax.ShapeDtypeStruct(grad.shape, f32),
        input_output_aliases={0: 0},
        name="add_rim",
    )(grad, rim)


def flat_rows():
    starts, at = {}, 0
    for name, shape in param_layout():
        starts[name] = at
        at += math.prod(shape) // C
    return starts, at


def unpack_kernel(
    slots, near, far, vecs, embed_w, q_w, kv_w, sr_w, proj_w, fc1, dwv, fc2h, flat
):
    half = near.shape[0]
    if half == 1:
        flat[0 : near.shape[1], :] = near[0].astype(f32)
    else:
        rows = (flat.shape[0] - SPARE) // (2 * half)
        first = slots[half] == 0
        for s in range(half):
            here, there = near[slots[s]][:rows], far[slots[s]][:rows]
            even, odd = 2 * s * rows, (2 * s + 1) * rows
            flat[even : even + rows, :] = jnp.where(first, here, there).astype(f32)
            flat[odd : odd + rows, :] = jnp.where(first, there, here).astype(f32)
    at, _ = flat_rows()

    def take(name, start, count):
        return flat[at[name] + start : at[name] + start + count, :]

    for i, name in enumerate(VEC_NAMES):
        vecs[i : i + 1, :] = take(name, 0, 1)
    vecs[len(VEC_NAMES) :, :] = jnp.zeros((16 - len(VEC_NAMES), C), f32)
    for a in range(3):
        embed_w[a * C : (a + 1) * C, :] = take("embed_w", a * 3 * C_IN + C_IN, C).astype(bf16)
        left = take("embed_w", a * 3 * C_IN, C_IN)
        embed_w[(3 + a) * C : (4 + a) * C, :] = jnp.concatenate(
            [jnp.zeros_like(left), left], axis=0
        ).astype(bf16)
    q_w[...] = take("q_w", 0, C).astype(bf16)
    kv_w[:, :C] = take("k_w", 0, C).astype(bf16)
    kv_w[:, C:] = take("v_w", 0, C).astype(bf16)
    sr_w[...] = take("sr_w", 0, 16 * C).astype(bf16)
    proj_w[...] = take("proj_w", 0, C).astype(bf16)
    fc2h[...] = (take("fc2_w", 0, FF) * 0.5).astype(bf16)
    dwv[...] = jnp.zeros_like(dwv)
    for c in range(FF // C):
        lanes = slice(c * C, (c + 1) * C)
        fc1[:, lanes] = flat[pl.ds(at["fc1_w"] + c, C, stride=FF // C), :].astype(bf16)
        for k in range(9):
            dwv[k : k + 1, lanes] = take("dw_w", k * (FF // C) + c, 1)
            dwv[16 + k : 17 + k, lanes] = take("fc1_b", c, 1)
        dwv[9:10, lanes] = take("dw_b", c, 1)
    dwv[25:26, :] = jnp.ones((1, FF), f32)


def unpack_call(slots, total, near, far):
    vmem_block = pl.BlockSpec(memory_space=pltpu.VMEM)
    sds = jax.ShapeDtypeStruct
    shapes = [
        sds((16, C), f32),
        sds((KEMB, C), bf16),
        sds((C, C), bf16),
        sds((C, 2 * C), bf16),
        sds((16 * C, C), bf16),
        sds((C, C), bf16),
        sds((C, FF), bf16),
        sds((32, FF), f32),
        sds((FF, C), bf16),
    ]
    return pl.pallas_call(
        unpack_kernel,
        in_specs=[pl.BlockSpec(memory_space=pltpu.SMEM), vmem_block, vmem_block],
        out_specs=[vmem_block] * len(shapes),
        out_shape=shapes,
        scratch_shapes=[pltpu.VMEM((total + SPARE, C), f32)],
        compiler_params=pltpu.CompilerParams(vmem_limit_bytes=VMEM_LIMIT),
        name="unpack",
    )(
        slots,
        pltpu.with_memory_space_constraint(near, pltpu.VMEM),
        pltpu.with_memory_space_constraint(far, pltpu.VMEM),
    )


def pack_into(
    slots, gemb, gvec_emb, gvec_att, gqw, gkv, gsr, gproj, gfc1, gdw, gfc2t, gfc2b,
    own, other, flat,
):
    at, used = flat_rows()

    def put(name, start, value):
        flat[at[name] + start : at[name] + start + value.shape[0], :] = value

    def vec_row(ref, k):
        return jnp.sum(ref[k], axis=0, keepdims=True)

    emb = gemb[...].T
    for a in range(3):
        put("embed_w", a * 3 * C_IN + C_IN, emb[a * C : (a + 1) * C])
        put("embed_w", a * 3 * C_IN, emb[(3 + a) * C + C_IN : (4 + a) * C])
    for k, name in enumerate(
        ("srn_g", "srn_b", "sr_b", "norm1_g", "norm1_b", "embed_g", "embed_beta", "embed_b")
    ):
        put(name, 0, vec_row(gvec_emb, k))
    for k, name in enumerate(("norm2_g", "norm2_b", "proj_b", "q_b", "v_b")):
        put(name, 0, vec_row(gvec_att, k))
    put("q_w", 0, gqw[...])
    put("k_w", 0, gkv[:, :C])
    put("v_w", 0, gkv[:, C:])
    put("sr_w", 0, gsr[...])
    put("proj_w", 0, gproj[...])
    put("fc2_b", 0, jnp.sum(gfc2b[...], axis=0, keepdims=True))
    put("fc2_w", 0, gfc2t[...].T)
    for c in range(FF // C):
        lanes = slice(c * C, (c + 1) * C)
        flat[pl.ds(at["fc1_w"] + c, C, stride=FF // C), :] = gfc1[:, lanes]
        for k in range(9):
            put("dw_w", k * (FF // C) + c, gdw[k : k + 1, lanes])
        put("dw_b", c, gdw[9:10, lanes])
        put("fc1_b", c, gdw[10:11, lanes])
    total = flat.shape[0] - SPARE
    flat[used:total, :] = jnp.zeros((total - used, C), f32)
    if other is None:
        own[0] = flat[0:total, :]
        return
    rows = total // (2 * own.shape[0])
    blank = jnp.zeros((own.shape[1] - rows, C), f32)
    first = slots[own.shape[0]] == 0
    for s in range(own.shape[0]):
        even = flat[2 * s * rows : (2 * s + 1) * rows, :]
        odd = flat[(2 * s + 1) * rows : (2 * s + 2) * rows, :]
        here, there = jnp.where(first, even, odd), jnp.where(first, odd, even)
        own[slots[s]] = jnp.concatenate([here, blank], axis=0)
        other[slots[s]] = jnp.concatenate([there, blank], axis=0).astype(bf16)


def other_core(block):
    size = lax.axis_size("rows")
    return lax.ppermute(block, "rows", [(i, i ^ 1) for i in range(size)])


def along_z(block, distance):
    size = lax.axis_size("rows")
    chain = size // 2
    route = [(i, 2 * ((i // 2 + distance) % chain) + i % 2) for i in range(size)]
    return lax.ppermute(block, "rows", route)


def batch_partner(index, k, size):
    return index ^ k if size & (size - 1) == 0 else (index + k) % size


def along_batch(block, k):
    size = lax.axis_size("batch")
    return lax.ppermute(block, "batch", [(i, batch_partner(i, k, size)) for i in range(size)])


def batch_source(k, size):
    return k if size & (size - 1) == 0 else (size - k) % size


def gather_chain(block):
    return jnp.stack([block] + [along_z(block, k) for k in range(1, lax.axis_size("rows") // 2)])


def z_partner(block, k):
    size = lax.axis_size("rows")
    return lax.ppermute(block, "rows", [(i, 2 * ((i // 2) ^ k) + i % 2) for i in range(size)])


def sum_over_devices(value):
    chain, batches = lax.axis_size("rows") // 2, lax.axis_size("batch")
    if chain & (chain - 1) or batches & (batches - 1):
        return lax.psum(value, ("batch", "rows"))
    value = value + other_core(value)
    for size, move in ((chain, z_partner), (batches, along_batch)):
        parts = [value] + [move(value, k) for k in range(1, size)]
        while len(parts) > 1:
            parts = [parts[i] + parts[i + 1] for i in range(0, len(parts), 2)]
        value = parts[0]
    return value


def per_step(count, wanted):
    return max(n for n in range(1, wanted + 1) if count % n == 0)


def shift_rows(block, distance):
    size = lax.axis_size("rows")
    route = [(i, i + distance) for i in range(size) if 0 <= i + distance < size]
    return lax.ppermute(block, "rows", route)


def shards(
    features,
    cotangent,
    crop_ids,
    pooled_ids,
    master_weights,
    first_moment,
    second_moment,
    weight_average,
):
    canvases, double_rows, grid_cols, pair_ch = features.shape
    grid_rows = double_rows // 2
    pool_rows, pool_cols = grid_rows // 4, grid_cols // 4
    tokens = grid_rows * grid_cols

    chain, batches = lax.axis_size("rows") // 2, lax.axis_size("batch")
    pieces = 2 * chain * batches
    part_len = master_weights.shape[0]
    total_params = part_len * pieces
    low = master_weights.astype(bf16)
    aligned = part_len % C == 0
    padded_rows = (part_len // C + 7) // 8 * 8
    if aligned:
        low = low.reshape(part_len // C, C)
        low = jnp.pad(low, ((0, padded_rows - part_len // C), (0, 0)))
    low = gather_chain(low)
    low = jnp.stack([low] + [along_batch(low, k) for k in range(1, batches)])
    row_index, batch_index = lax.axis_index("rows"), lax.axis_index("batch")
    core, z_index = row_index % 2, row_index // 2
    piece = jnp.arange(pieces, dtype=jnp.int32)
    piece_core, piece_z = piece % 2, piece // 2 % chain
    piece_batch = piece // (2 * chain)
    if batches & (batches - 1) == 0:
        batch_slot = piece_batch ^ batch_index
    else:
        batch_slot = (batch_index - piece_batch) % batches
    half_slot = batch_slot * chain + (z_index - piece_z) % chain
    slots = (piece_core ^ core) * (batches * chain) + half_slot
    pair_slots = jnp.concatenate([half_slot[::2], core[None]])
    feat = features.reshape(canvases, grid_rows, 2, grid_cols, pair_ch)
    rim = shift_rows(features[:, double_rows - 1], 1)
    above_ids = shift_rows(pooled_ids[:, pool_rows - 1], 1)
    above_ids = jnp.where(row_index == 0, -1, above_ids)
    below_ids = shift_rows(pooled_ids[:, 0], -1)
    below_ids = jnp.where(row_index == 2 * chain - 1, -1, below_ids)
    idr = jnp.concatenate(
        [
            jnp.repeat(above_ids, 4, axis=1),
            crop_ids.reshape(canvases, tokens),
            jnp.repeat(below_ids, 4, axis=1),
        ],
        axis=1,
    )
    extended = tokens + 2 * grid_cols
    idr = jnp.pad(idr, ((0, 0), (0, lane_pad(extended) - extended)), constant_values=-1)
    idr = idr[:, None]
    own_ids = pooled_ids.reshape(canvases, pool_rows * pool_cols)
    own_ids = jnp.pad(own_ids, ((0, 0), (0, C - pool_rows * pool_cols)))[:, None]

    every = Group(canvases, 0)
    hm, vm = near_masks_call(every, grid_rows, grid_cols, idr)
    low, hm, vm, own_ids, rim, pair_slots = lax.optimization_barrier(
        (low, hm, vm, own_ids, rim, pair_slots)
    )
    far_low = other_core(low)
    if aligned:
        low = low.reshape(pieces // 2, padded_rows, C)
        far_low = far_low.reshape(low.shape)
    else:
        both = jnp.stack([low, far_low]).reshape(pieces, part_len)
        low = jnp.take(both, slots, axis=0).reshape(1, total_params // C, C)
        far_low = low[:, :8]
    vecs, embed_w, q_w, kv_w, sr_w, proj_w, fc1, dwv, fc2h = unpack_call(
        pair_slots, total_params // C, low, far_low
    )

    cot = cotangent.reshape(canvases, tokens, C)
    groups = [every]
    embed_group = Group(canvases, 0, per_step(canvases, EMBED_PER))
    attend_group = Group(canvases, 0, per_step(canvases, ATTEND_PER))
    attend_back_group = Group(canvases, 0, per_step(canvases, ATTEND_BACK_PER))
    embed_back_group = Group(canvases, 0, per_step(canvases, EMBED_BACK_PER))
    embedded, chains, gathered = [], [], []
    for group in groups:
        embedded.append(embed_call(embed_group, feat, rim, hm, vm, own_ids, vecs, embed_w, q_w, sr_w))
        chains.append(gather_chain(embedded[-1][6]))
    late_idr, _ = lax.optimization_barrier((idr, embedded[-1][6]))
    token_masks = token_masks_call(every, grid_rows, grid_cols, late_idr)
    chains[-1], token_masks = lax.optimization_barrier((chains[-1], token_masks))
    q_hot, aug, aug_rows = token_masks
    gathered = [(near, other_core(near)) for near in chains]
    attended, halos = [], []
    for group, (_, base, _, q, _, _, _, _), (near, far) in zip(groups, embedded, gathered):
        attended.append(attend_call(attend_group, grid_cols, q, near, far, q_hot, base, vecs, kv_w, proj_w))
        _, _, _, _, _, head, tail = attended[-1]
        halos.append((shift_rows(tail, 1), shift_rows(head, -1)))
    layer_out, fed, back_halos = (), [], []
    for group, (_, _, _, att, sec, _, _), (top, bot) in zip(groups, attended, halos):
        wide = Group(group.count, group.first, per_step(canvases, MLP_PER))
        out = mlp_call(
            wide, sec, top, bot, hm, vm, aug, aug_rows, cot, att, fc1, dwv, fc2h, vecs, layer_out
        )
        layer_out = (out[0],)
        fed.append(out)
        back_halos.append((shift_rows(out[3], 1), shift_rows(out[2], -1)))
    backs, pool_parts = [], []
    for g, group in enumerate(groups):
        emb, _, normed, q, blk, red, _, patches = embedded[g]
        exp_scores, mix, inv, att = attended[g][:4]
        out = attend_back_call(
            attend_back_group, fed[g][1], *back_halos[g], att, cot, mix, inv, exp_scores, q, normed,
            *gathered[g], vecs, kv_w, proj_w,
        )
        backs.append(out)
        mine, theirs = out[2], other_core(out[3])
        pool_parts.append([mine, theirs])
        for k in range(1, chain):
            both = mine[k].astype(f32) + theirs[k].astype(f32)
            pool_parts[-1].append(along_z(both.astype(bf16), -k))
    emb, _, _, _, blk, red, _, patches = embedded[0]
    gatt, gq, _, _, g_proj_w, g_kv_w, g_q_w, gvec_att = backs[0]
    half = (pieces // 2, padded_rows, C) if aligned else (1, total_params // C, C)
    g_in, grim, own, *other = embed_back_call(
        embed_back_group, feat, pool_parts[0], red, emb, gatt, gq, blk, patches, hm, vm,
        vecs, embed_w, q_w, sr_w,
        pair_slots, [gvec_att, g_q_w, g_kv_w, g_proj_w, *fed[0][4:]], total_params // C, half,
    )
    layer_out = layer_out[0]
    input_grad = add_rim_call(g_in, shift_rows(grim, -1))

    if aligned:
        own = own.reshape(batches, chain, padded_rows, C)
        other = other[0].reshape(batches, chain, padded_rows, C)
    else:
        order = jnp.zeros((pieces,), jnp.int32).at[slots].set(piece)
        both = jnp.take(own.reshape(pieces, part_len), order, axis=0)
        both = both.reshape(2, batches, chain, part_len)
        own, other = both[0], both[1].astype(bf16)
    own = own + other_core(other).astype(f32)
    own = sum(
        [
            along_batch(own[batch_source(k, batches)].astype(bf16), k).astype(f32)
            for k in range(1, batches)
        ],
        own[0],
    )
    own, input_grad = lax.optimization_barrier((own, input_grad))
    input_grad = input_grad.reshape(features.shape)
    shard_grad = sum(
        [along_z(own[k].astype(bf16), -k).astype(f32) for k in range(1, chain)], own[0]
    )
    if aligned:
        squares = jnp.sum((shard_grad * shard_grad).reshape(-1, 8, C), axis=0)
    else:
        squares = jnp.broadcast_to(jnp.sum(shard_grad * shard_grad) / (8 * C), (8, C))
    square_sum = jnp.sum(sum_over_devices(squares))
    if aligned:
        shard_grad = shard_grad[: part_len // C]
    shard_grad = shard_grad.reshape(part_len)
    grad_norm = jnp.sqrt(square_sum)
    clip_limit = math.sqrt(total_params)
    clipped = shard_grad * (clip_limit / jnp.maximum(grad_norm, clip_limit))
    new_first = BETA_ONE * first_moment + (1.0 - BETA_ONE) * clipped
    new_second = BETA_TWO * second_moment + (1.0 - BETA_TWO) * clipped * clipped
    first_hat = new_first / (1.0 - BETA_ONE**UPDATES)
    second_hat = new_second / (1.0 - BETA_TWO**UPDATES)
    new_weights = master_weights * (1.0 - LEARN_RATE * DECAY_RATE) - LEARN_RATE * first_hat / (
        jnp.sqrt(second_hat) + ADAM_EPS
    )
    new_average = AVERAGE_KEEP * weight_average + (1.0 - AVERAGE_KEEP) * new_weights
    layer_out = layer_out.reshape(cotangent.shape)
    return (layer_out, input_grad, grad_norm, new_first, new_second, new_weights, new_average)


def solution(mesh):
    placed = (
        P("batch", "rows", None, None),
        P("batch", "rows", None, None),
        P("batch", "rows", None),
        P("batch", "rows", None),
        P(("batch", "rows")),
        P(("batch", "rows")),
        P(("batch", "rows")),
        P(("batch", "rows")),
    )
    return jax.shard_map(
        shards,
        mesh=mesh,
        in_specs=placed,
        out_specs=(
            P("batch", "rows", None, None),
            P("batch", "rows", None, None),
            P(),
            P(("batch", "rows")),
            P(("batch", "rows")),
            P(("batch", "rows")),
            P(("batch", "rows")),
        ),
        check_vma=False,
    )
```
